32 devices in a mesh: nodes: 8 (over z, y), cblk: 4 (over x, core).
Axes of the slice: x: 2, y: 2, z: 4, core: 2. Of those that a mesh axis runs over, the one named last changes fastest.
Arguments:
- sens: bfloat16 [8192, 128], P(('nodes', 'cblk')), may hold values from -1.5 to 1.5
- dest_owner: int32 [8192, 1], P(('nodes', 'cblk')), may hold values from 0 to 3; in each aligned block of 256 rows (0 to 255, 256 to 511, ...) at most 128 rows name the same one
- dest_slot: int32 [8192], P(('nodes', 'cblk')), may hold values from 0 to 127
- coef_scale: float32 [4096], P(('nodes', 'cblk')), may hold values from 0.5 to 2
- centre_pos: bfloat16 [3, 4096], P(None, ('nodes', 'cblk')), may hold values from 0 to 1
- node_pos: bfloat16 [3, 65536], P(None, ('nodes', 'cblk')), may hold values from 0 to 1
- support: int32 [128, 4], P(('nodes', 'cblk')), may hold values 0 or 1
Outputs:
- morph: float32 [65536, 128], P(('nodes', 'cblk'))
The draws below stay inside these ranges and needn't reach their ends.
Inputs may be any that keep to these rules, and one draw needn't show every extreme that they name: `dest_owner`: among the rows of one device no block is named by more than 128 rows, and in every draw some device names one block exactly 128 times.
All inputs are finite; a program needn't handle non-finite values. No bound on the sum of `support` on one device may be relied on, other than what follows from the above.
Results may differ from the reference program's by a relative error of at most 0.0042.
Values may be sent and summed in bfloat16 or wider, within the bound.
No kernel may reach another device: no remote copies, remote signals or barrier semaphores. Data moves between devices by JAX's collectives and lax.ppermute only.
A program may use at most 64 MiB of HBM per device.

```python
import math
import jax
import jax.numpy as jnp
import numpy as np
from jax import lax

FEATS = 128
CEN_DEV = 128
ROW_DEV = 256
TILE = 512
CAP = 128
NBLK = 4
NCEN = 4096
ROWS = 8192
NODES = 65536
NTILES = 128


def place_ends(result, key, low, largest):
    place = [jax.random.randint(jax.random.fold_in(key, axis), (), 0, length) for axis, length in enumerate(result.shape)]
    widest = result.shape.index(max(result.shape))
    neighbour = place[:widest] + [(place[widest] + 1) % result.shape[widest]] + place[widest + 1:]
    return result.at[tuple(place)].set(low).at[tuple(neighbour)].set(largest)


def block_levels(rng, dims, shards, least, largest):
    gain, own = 1.0, jax.random.fold_in(rng, 6)
    for dim, shards_of in shards:
        draws = jnp.exp(jax.random.uniform(jax.random.fold_in(own, dim), (shards_of,), jnp.float32, least / len(shards), largest / len(shards)))
        gain = gain * jnp.repeat(draws, dims[dim] // shards_of).reshape([-1 if axis == dim else 1 for axis in range(len(dims))])
    return gain


def assign_block(own_key, own, number, rows, count, top, most, lean):
    order = jax.random.permutation(own_key, count)
    heavy_load, usual = portions_of(count, rows * top, most, lean, True), portions_of(count, rows * top, most, lean, False)
    places = jnp.arange(count)

    def named(sizes, turn):
        used = int((sizes > 0).sum())
        fixed = max(1, used // 4)
        passed = fixed + (places - fixed + turn * (used - fixed)) % max(1, count - fixed)
        return jnp.zeros((count,), jnp.int32).at[order[jnp.where(places < fixed, places, passed)]].set(jnp.asarray(sizes, jnp.int32))

    sizes = jnp.where(number % 4 == 0, named(heavy_load, number // 4), named(usual, number - number // 4 - 1))
    mixed = jax.random.permutation(jax.random.fold_in(own, 3), count)
    giver, receiver = mixed[0:count // 2 * 2:2], mixed[1:count // 2 * 2:2]
    slack = jnp.minimum(sizes[giver] - 1, most - sizes[receiver]) // 2
    slack = jnp.where((giver == order[0]) | (receiver == order[0]) | (sizes[receiver] == 0), 0, jnp.maximum(slack, 0))
    passed = jax.random.randint(jax.random.fold_in(own, 4), (count // 2,), 0, 1 << 20) % (slack + 1)
    sizes = sizes.at[giver].add(-passed).at[receiver].add(passed)
    items = jnp.searchsorted(jnp.cumsum(sizes), jnp.arange(rows * top), side="right").astype(jnp.int32)
    listing = items.reshape(top, rows).T
    listing = listing[jax.random.permutation(jax.random.fold_in(own, 1), rows)]
    turn = jax.random.randint(jax.random.fold_in(own, 2), (rows, 1), 0, top)
    return jnp.take_along_axis(listing, (jnp.arange(top)[None, :] + turn) % top, axis=1)


def portions_of(count, total, limit, lean, full):
    loads = [(1 << 20) // math.isqrt(standing ** lean) + 1 for standing in range(1, count + 1)]
    largest = limit if full else min(limit, max(-(-total // count), total * loads[0] // sum(loads)))
    least = 1 if total - largest >= count - 1 else 0
    counts, spare = [largest] + [least] * (count - 1), total - largest - least * (count - 1)
    while spare > 0:
        free = [i for i in range(1, count) if counts[i] < largest] or [i for i in range(1, count) if counts[i] < limit]
        mass, budget = sum([loads[i] for i in free]), spare
        for i in free:
            more = min(limit - counts[i], max(1, budget * loads[i] // mass), spare)
            counts[i] = counts[i] + more
            spare = spare - more
    return np.array(counts)


def centred(own_key, shape, scale, limit, shards=(), kind=jnp.bfloat16):
    drawn = scale * jax.random.normal(own_key, shape, jnp.float32)
    if shards:
        drawn = drawn * block_levels(own_key, shape, shards, -0.22, 0.18)
    return jnp.clip(drawn, -limit, limit).astype(kind)


def setup_inputs(seed: int = 0) -> dict:
    splits = jax.random.split(jax.random.key(seed), 8)
    sens = centred(splits[0], (ROWS, FEATS), 0.25, 1.5, ((0, 32),))
    dest_owner_keys = jax.random.split(jax.random.fold_in(splits[1], 1), ROWS // ROW_DEV)
    dest_owner_turns = jax.random.permutation(jax.random.fold_in(splits[1], 3), ROWS // ROW_DEV)
    dest_owner = jax.vmap(lambda own, number: assign_block(jax.random.fold_in(splits[1], 2), own, number, ROW_DEV, NBLK, 1, CAP, 2))(dest_owner_keys, dest_owner_turns).reshape((ROWS, 1))
    dest_slot = place_ends(jax.random.randint(splits[2], (ROWS,), 0, CEN_DEV), jax.random.fold_in(splits[2], 1), 0, CEN_DEV - 1).astype(jnp.int32)
    coef_scale = jnp.clip(jnp.exp(math.log(2.0) - 1.3862944 * jax.random.uniform(splits[3], (NCEN,), jnp.float32) ** block_levels(splits[3], (NCEN,), ((0, 32),), -0.2, 0.2)), 0.5, 2.0)
    centre_pos = jnp.clip(1.0 * jax.random.uniform(splits[4], (3, NCEN), jnp.float32) ** block_levels(splits[4], (3, NCEN), ((1, 32),), -0.2, 0.2), 0.0, 1.0).astype(jnp.bfloat16)
    node_pos = jnp.clip(1.0 * jax.random.uniform(splits[5], (3, NODES), jnp.float32) ** block_levels(splits[5], (3, NODES), ((1, 32),), -0.2, 0.2), 0.0, 1.0).astype(jnp.bfloat16)
    support = place_ends((jax.random.randint(splits[6], (NTILES, NBLK), 0, 4) < 3).astype(jnp.int32), jax.random.fold_in(splits[6], 1), 0, 1)
    return dict(sens=sens, dest_owner=dest_owner, dest_slot=dest_slot, coef_scale=coef_scale, centre_pos=centre_pos, node_pos=node_pos, support=support)


support_radius = 0.3

def wendland(dist):
    base = jnp.maximum(1.0 - dist / support_radius, 0.0)
    square = base * base
    return square * square * (5.0 - 4.0 * base)

def reference(sens, dest_owner, dest_slot, coef_scale, centre_pos, node_pos, support):
    row_ids = jnp.arange(ROWS, dtype=jnp.int32)
    column = row_ids // ROW_DEV // NBLK
    target = ((column * NBLK + dest_owner[:, 0]) * CEN_DEV + dest_slot).astype(jnp.int32)
    sums = jax.ops.segment_sum(sens.astype(jnp.float32), target, num_segments=NCEN)
    coef = (coef_scale[:, None] * sums).astype(jnp.bfloat16)
    block_of = (jnp.arange(NCEN, dtype=jnp.int32) // CEN_DEV % NBLK).astype(jnp.int32)
    centres = centre_pos.astype(jnp.float32)
    mask_table = support.astype(jnp.float32)[:, block_of]

    def one_tile(index):
        points = lax.dynamic_slice_in_dim(node_pos, index * TILE, TILE, 1).astype(jnp.float32)
        square = (points[0][:, None] - centres[0][None, :]) ** 2
        square = square + (points[1][:, None] - centres[1][None, :]) ** 2
        square = square + (points[2][:, None] - centres[2][None, :]) ** 2
        kernel = wendland(jnp.sqrt(square))
        mask_row = lax.dynamic_slice_in_dim(mask_table, index, 1, 0)
        weight = (kernel * mask_row).astype(jnp.bfloat16)
        return jnp.dot(weight, coef, preferred_element_type=jnp.float32)
    blocks = lax.map(one_tile, jnp.arange(NTILES, dtype=jnp.int32))
    return blocks.reshape(NODES, FEATS)
```

```python
import functools

import jax
import jax.numpy as jnp
from jax import lax
from jax.experimental import pallas as pl
from jax.experimental.pallas import tpu as pltpu
from jax.sharding import PartitionSpec as P

LANES = 128
META = 8
EXTRA = 16
DEPTH = 32
FAR = 64.0
SUPPORT_RADIUS = 0.3
GAIN = 16.0 / (SUPPORT_RADIUS * SUPPORT_RADIUS)


def split3(value):
    high = value.astype(jnp.bfloat16).astype(jnp.float32)
    rest = value - high
    middle = rest.astype(jnp.bfloat16).astype(jnp.float32)
    return high, middle, rest - middle


def stack_rows(rows, width):
    rows = rows + [jnp.zeros((1, width), jnp.float32)] * (DEPTH - len(rows))
    return jnp.concatenate(rows, axis=0).astype(jnp.bfloat16)


def node_kernel(core_ref, support_ref, pos_ref, out_ref, *, blocks):
    count = pos_ref.shape[1]
    tiles = support_ref.shape[0]
    width = count // tiles
    core = core_ref[0]
    for tile in range(tiles):
        cols = pl.ds(tile * width, width)
        points = [pos_ref[k : k + 1, cols].astype(jnp.float32) for k in range(3)]
        norm = GAIN * (points[0] * points[0] + points[1] * points[1] + points[2] * points[2])
        ones = jnp.ones_like(norm)
        rows = points * 3 + list(split3(norm)) + [ones] * 3
        for k in range(blocks):
            place = lax.rem(core * (blocks // 2) + k, blocks)
            off = (1 - support_ref[tile, place]).astype(jnp.float32)
            rows.append(ones * off)
        out_ref[cols, :] = jnp.swapaxes(stack_rows(rows, width), 0, 1)


def coef_kernel(where_ref, *refs, blocks):
    rows_refs, meta_refs = refs[:blocks], refs[blocks : 2 * blocks]
    own_ref, other_ref, metas = refs[2 * blocks :]
    row_count = rows_refs[0].shape[0]
    me = where_ref[0]
    core = where_ref[1]
    half = blocks // 2 * LANES
    for s in range(blocks):
        metas[s] = meta_refs[s][...]
    groups = row_count // LANES
    start = core * half
    place = lax.broadcasted_iota(jnp.int32, (blocks * LANES, LANES), 0) + start
    place = lax.rem(place, blocks * LANES).astype(jnp.float32)
    sums = jnp.zeros((blocks * LANES, LANES), jnp.float32)
    hits = []
    for s in range(blocks):
        for g in range(groups):
            target = metas[s, 4 + g : 5 + g, :]
            hits.append((place == target).astype(jnp.float32).astype(jnp.bfloat16))
    for s in range(blocks):
        picked = jnp.concatenate(hits[s * groups : (s + 1) * groups], axis=1)
        sums = sums + jnp.dot(picked, rows_refs[s][...], preferred_element_type=jnp.float32)
    pos_rows = []
    for k in range(blocks):
        block = lax.rem(core * (blocks // 2) + k, blocks)
        meta = metas[block ^ me]
        scale = jnp.swapaxes(jnp.broadcast_to(meta[3:4, :], (8, LANES)), 0, 1)[:, 0:1]
        coef = (scale * sums[k * LANES : (k + 1) * LANES, :]).astype(jnp.bfloat16)
        if k < blocks // 2:
            own_ref[k * LANES : (k + 1) * LANES, :] = coef
        else:
            other_ref[k * LANES - half : (k + 1) * LANES - half, :] = coef
        pos_rows.append(meta[0:3, :])
    pos_rows.append(jnp.zeros((EXTRA - 3 * blocks, LANES), jnp.float32))
    own_ref[half : half + EXTRA, :] = jnp.concatenate(pos_rows, axis=0).astype(jnp.bfloat16)


def centre_features(chunk_ref, half, blocks, out_ref, col):
    for k in range(blocks):
        pos = chunk_ref[half : half + EXTRA, :].astype(jnp.float32)[3 * k : 3 * k + 3, :]
        axes = [pos[d : d + 1, :] for d in range(3)]
        norm = GAIN * (axes[0] * axes[0] + axes[1] * axes[1] + axes[2] * axes[2])
        parts = [split3(-2.0 * GAIN * axis) for axis in axes]
        ones = jnp.ones_like(norm)
        rows = [parts[d][p] for p in range(3) for d in range(3)] + [ones] * 3 + list(split3(norm))
        rows += [ones * (FAR if k == b else 0.0) for b in range(blocks)]
        out_ref[:, col + k * LANES : col + (k + 1) * LANES] = stack_rows(rows, LANES)


def morph_kernel(*refs, blocks, chunks, first, last, tile):
    feats_ref = refs[0]
    refs = refs[1:]
    if not first:
        acc_ref, refs = refs[0], refs[1:]
    own_refs, other_refs = refs[:chunks], refs[chunks : 2 * chunks]
    out_ref, cen_ref = refs[2 * chunks :]
    half = blocks // 2 * LANES
    for t in range(chunks):
        centre_features(own_refs[t], half, blocks, cen_ref, 2 * half * t)

    def step(index, carry):
        rows = pl.ds(pl.multiple_of(index * tile, tile), tile)
        feats = feats_ref[rows, :]
        total = jnp.zeros((tile, LANES), jnp.float32) if first else acc_ref[rows, :]
        for t in range(chunks):
            for h, coef_ref in enumerate((own_refs[t], other_refs[t])):
                col = 2 * half * t + half * h
                square = jnp.dot(
                    feats, cen_ref[:, col : col + half], preferred_element_type=jnp.float32
                )
                square = jnp.maximum(square, 1e-30)
                reach = square * lax.rsqrt(square)
                base = jnp.maximum(4.0 - reach, 0.0)
                base = base * base
                weight = (base * base * (reach + 1.0)).astype(jnp.bfloat16)
                total = total + jnp.dot(
                    weight, coef_ref[0:half, :], preferred_element_type=jnp.float32
                )
        out_ref[rows, :] = total * (1.0 / 256.0) if last else total
        return carry

    lax.fori_loop(0, feats_ref.shape[0] // tile, step, 0)


def vmem_specs(count):
    return [pl.BlockSpec(memory_space=pltpu.VMEM) for _ in range(count)]


def smem_specs(count):
    return [pl.BlockSpec(memory_space=pltpu.SMEM) for _ in range(count)]


def per_device(sens, dest_owner, dest_slot, coef_scale, centre_pos, node_pos, support):
    blocks = lax.axis_size("cblk")
    columns = lax.axis_size("nodes")
    row_count = sens.shape[0]
    groups = row_count // LANES
    half = blocks // 2 * LANES
    node_count = node_pos.shape[1]
    me = lax.axis_index("cblk").astype(jnp.int32)
    core = me & 1
    where = jnp.stack([me, core])

    target = (dest_owner[:, 0] * LANES + dest_slot).astype(jnp.float32).reshape(groups, LANES)
    meta = jnp.concatenate(
        [centre_pos.astype(jnp.float32), coef_scale[None, :], target]
        + [jnp.zeros((META - 4 - groups, LANES), jnp.float32)],
        axis=0,
    )

    def swap(value, axis, size, mask):
        return lax.ppermute(value, axis, [(i, i ^ mask) for i in range(size)])

    rows, metas = [sens], [meta]
    order = [0]
    mask = blocks // 2
    while mask:
        rows = rows + [swap(value, "cblk", blocks, mask) for value in rows]
        metas = metas + [swap(value, "cblk", blocks, mask) for value in metas]
        order = order + [s ^ mask for s in order]
        mask //= 2
    rows = [rows[order.index(s)] for s in range(blocks)]
    metas = [metas[order.index(s)] for s in range(blocks)]

    feats = pl.pallas_call(
        functools.partial(node_kernel, blocks=blocks),
        in_specs=smem_specs(2) + vmem_specs(1),
        out_specs=vmem_specs(1)[0],
        out_shape=jax.ShapeDtypeStruct((node_count, DEPTH), jnp.bfloat16),
        name="node_features",
    )(core[None], support, node_pos)

    own, other = pl.pallas_call(
        functools.partial(coef_kernel, blocks=blocks),
        in_specs=smem_specs(1) + vmem_specs(2 * blocks),
        out_specs=vmem_specs(2),
        out_shape=[
            jax.ShapeDtypeStruct((half + EXTRA, LANES), jnp.bfloat16),
            jax.ShapeDtypeStruct((half, LANES), jnp.bfloat16),
        ],
        scratch_shapes=[pltpu.VMEM((blocks, META, LANES), jnp.float32)],
        name="coefficients",
    )(where, *rows, *metas)

    def morph(total, chunks, last):
        count = len(chunks)
        first = total is None
        operands = [feats] + ([] if first else [total])
        operands += [chunk[0] for chunk in chunks] + [chunk[1] for chunk in chunks]
        work = node_count * count * 2 * half
        return pl.pallas_call(
            functools.partial(
                morph_kernel, blocks=blocks, chunks=count, first=first, last=last, tile=256
            ),
            in_specs=vmem_specs(len(operands)),
            out_specs=vmem_specs(1)[0],
            out_shape=jax.ShapeDtypeStruct((node_count, LANES), jnp.float32),
            scratch_shapes=[pltpu.VMEM((DEPTH, 2 * half * count), jnp.bfloat16)],
            input_output_aliases={} if first else {1: 0},
            cost_estimate=pl.CostEstimate(
                flops=work * 600, transcendentals=work, bytes_accessed=node_count * LANES * 8
            ),
            name="morph",
        )(*operands)

    total = None
    chunks = [(own, other)]
    fresh = chunks
    mask = columns // 2
    while mask:
        arrived = [swap(chunk[0], "nodes", columns, mask) for chunk in chunks]
        total = morph(total, fresh, False)
        fresh = [(value, swap(value, "cblk", blocks, 1)) for value in arrived]
        chunks = chunks + fresh
        mask //= 2
    return morph(total, fresh, True)


def solution(mesh):
    placed = (
        P(("nodes", "cblk"), None),
        P(("nodes", "cblk"), None),
        P(("nodes", "cblk")),
        P(("nodes", "cblk")),
        P(None, ("nodes", "cblk")),
        P(None, ("nodes", "cblk")),
        P(("nodes", "cblk"), None),
    )
    return jax.shard_map(
        per_device,
        mesh=mesh,
        in_specs=placed,
        out_specs=P(("nodes", "cblk"), None),
        check_vma=False,
    )
```

```python
import functools

import jax
import jax.numpy as jnp
from jax import lax
from jax.experimental import pallas as pl
from jax.experimental.pallas import tpu as pltpu
from jax.sharding import PartitionSpec as P

LANES = 128
EXTRA = 16
DEPTH = 32
FAR = 64.0
VMEM_LIMIT = 16 * 1024 * 1024
SUPPORT_RADIUS = 0.3
GAIN = 16.0 / (SUPPORT_RADIUS * SUPPORT_RADIUS)


def split3(value):
    high = value.astype(jnp.bfloat16).astype(jnp.float32)
    rest = value - high
    middle = rest.astype(jnp.bfloat16).astype(jnp.float32)
    return high, middle, rest - middle


def stack_rows(rows, width):
    rows = rows + [jnp.zeros((1, width), jnp.float32)] * (DEPTH - len(rows))
    return jnp.concatenate(rows, axis=0).astype(jnp.bfloat16)


def prepare_kernel(me_ref, support_ref, pos_ref, sens_ref, out_ref, rows_ref, *, blocks):
    count = pos_ref.shape[1]
    tiles = support_ref.shape[0]
    width = count // tiles
    core = me_ref[0] & 1
    rows_ref[...] = sens_ref[...]
    for tile in range(tiles):
        cols = pl.ds(tile * width, width)
        points = [pos_ref[k : k + 1, cols].astype(jnp.float32) for k in range(3)]
        norm = GAIN * (points[0] * points[0] + points[1] * points[1] + points[2] * points[2])
        ones = jnp.ones_like(norm)
        rows = points * 3 + list(split3(norm)) + [ones] * 3
        for k in range(blocks):
            place = lax.rem(core * (blocks // 2) + k, blocks)
            off = (1 - support_ref[tile, place]).astype(jnp.float32)
            rows.append(ones * off)
        out_ref[cols, :] = jnp.swapaxes(stack_rows(rows, width), 0, 1)


def coef_kernel(me_ref, *refs, blocks):
    rows_refs, owner_refs, slot_refs, scale_refs, pos_refs = (
        refs[blocks * n : blocks * (n + 1)] for n in range(5)
    )
    own_ref, other_ref, scales, points = refs[5 * blocks :]
    me = me_ref[0]
    core = me & 1
    half = blocks // 2 * LANES
    groups = rows_refs[0].shape[0] // LANES
    place = lax.broadcasted_iota(jnp.int32, (blocks * LANES, LANES), 0) + core * half
    place = place & (blocks * LANES - 1)
    sums = jnp.zeros((blocks * LANES, LANES), jnp.float32)
    for s in range(blocks):
        scales[s] = jnp.broadcast_to(scale_refs[s][...], (8, LANES))
        points[s] = pos_refs[s][...].astype(jnp.float32)
        target = owner_refs[s][...] * LANES + slot_refs[s][...]
        picked = jnp.concatenate(
            [
                (place == target[g : g + 1, :]).astype(jnp.float32).astype(jnp.bfloat16)
                for g in range(groups)
            ],
            axis=1,
        )
        sums = sums + jnp.dot(picked, rows_refs[s][...], preferred_element_type=jnp.float32)
    pos_rows = []
    for k in range(blocks):
        block = lax.rem(core * (blocks // 2) + k, blocks) ^ me
        scale = jnp.swapaxes(scales[block], 0, 1)[:, 0:1]
        coef = (scale * sums[k * LANES : (k + 1) * LANES, :]).astype(jnp.bfloat16)
        if k < blocks // 2:
            own_ref[k * LANES : (k + 1) * LANES, :] = coef
        else:
            other_ref[k * LANES - half : (k + 1) * LANES - half, :] = coef
        pos_rows.append(points[block])
    pos_rows.append(jnp.zeros((EXTRA - 3 * blocks, LANES), jnp.float32))
    own_ref[half : half + EXTRA, :] = jnp.concatenate(pos_rows, axis=0).astype(jnp.bfloat16)


def centre_features(chunk_ref, half, blocks, out_ref, col):
    for k in range(blocks):
        pos = chunk_ref[half : half + EXTRA, :].astype(jnp.float32)[3 * k : 3 * k + 3, :]
        axes = [pos[d : d + 1, :] for d in range(3)]
        norm = GAIN * (axes[0] * axes[0] + axes[1] * axes[1] + axes[2] * axes[2])
        parts = [split3(-2.0 * GAIN * axis) for axis in axes]
        ones = jnp.ones_like(norm)
        rows = [parts[d][p] for p in range(3) for d in range(3)] + [ones] * 3 + list(split3(norm))
        rows += [ones * (FAR if k == b else 0.0) for b in range(blocks)]
        out_ref[:, col + k * LANES : col + (k + 1) * LANES] = stack_rows(rows, LANES)


def morph_kernel(*refs, blocks, chunks, first, last, tile):
    feats_ref = refs[0]
    refs = refs[1:]
    if not first:
        acc_ref, refs = refs[0], refs[1:]
    own_refs, other_refs = refs[:chunks], refs[chunks : 2 * chunks]
    out_ref, cen_ref = refs[2 * chunks : 2 * chunks + 2]
    if last:
        done_ref, sems = refs[2 * chunks + 2 :]
    half = blocks // 2 * LANES
    for t in range(chunks):
        centre_features(own_refs[t], half, blocks, cen_ref, 2 * half * t)

    def leave(index):
        rows = pl.ds(pl.multiple_of(index * tile, tile), tile)
        return pltpu.make_async_copy(done_ref.at[rows, :], out_ref.at[rows, :], sems.at[index])

    def step(index, carry):
        rows = pl.ds(pl.multiple_of(index * tile, tile), tile)
        feats = feats_ref[rows, :]
        total = jnp.zeros((tile, LANES), jnp.float32) if first else acc_ref[rows, :]
        for t in range(chunks):
            for h, coef_ref in enumerate((own_refs[t], other_refs[t])):
                col = 2 * half * t + half * h
                square = jnp.dot(
                    feats, cen_ref[:, col : col + half], preferred_element_type=jnp.float32
                )
                square = jnp.maximum(square, 1e-30)
                reach = square * lax.rsqrt(square)
                base = jnp.maximum(4.0 - reach, 0.0)
                base = base * base
                weight = (base * base * (reach + 1.0)).astype(jnp.bfloat16)
                total = total + jnp.dot(
                    weight, coef_ref[0:half, :], preferred_element_type=jnp.float32
                )
        if last:
            done_ref[rows, :] = total * (1.0 / 256.0)
            leave(index).start()
        else:
            out_ref[rows, :] = total
        return carry

    steps = feats_ref.shape[0] // tile
    lax.fori_loop(0, steps, step, 0)
    if last:

        def settle(index, carry):
            leave(index).wait()
            return carry

        lax.fori_loop(0, steps, settle, 0)


def vmem_specs(count):
    return [pl.BlockSpec(memory_space=pltpu.VMEM) for _ in range(count)]


def resident(value):
    return pltpu.with_memory_space_constraint(value, pltpu.VMEM)


def smem_specs(count):
    return [pl.BlockSpec(memory_space=pltpu.SMEM) for _ in range(count)]


def per_device(sens, dest_owner, dest_slot, coef_scale, centre_pos, node_pos, support):
    blocks = lax.axis_size("cblk")
    columns = lax.axis_size("nodes")
    row_count = sens.shape[0]
    groups = row_count // LANES
    half = blocks // 2 * LANES
    node_count = node_pos.shape[1]
    tile = 256
    me = lax.axis_index("cblk").astype(jnp.int32)[None]

    def swap(value, axis, size, mask):
        return lax.ppermute(value, axis, [(i, i ^ mask) for i in range(size)])

    feats, local = pl.pallas_call(
        functools.partial(prepare_kernel, blocks=blocks),
        in_specs=smem_specs(2) + vmem_specs(2),
        out_specs=vmem_specs(2),
        out_shape=[
            pltpu.VMEM((node_count, DEPTH), jnp.bfloat16),
            pltpu.VMEM((row_count, LANES), jnp.bfloat16),
        ],
        cost_estimate=pl.CostEstimate(
            flops=node_count * 10000, transcendentals=0, bytes_accessed=node_count * 8
        ),
        compiler_params=pltpu.CompilerParams(vmem_limit_bytes=VMEM_LIMIT),
        name="prepare",
    )(me, support, node_pos, sens)

    sets = [
        (
            sens,
            dest_owner.reshape(groups, LANES),
            dest_slot.reshape(groups, LANES),
            coef_scale.reshape(1, LANES),
            centre_pos,
        )
    ]
    order = [0]
    mask = blocks // 2
    while mask:
        sets = sets + [tuple(swap(value, "cblk", blocks, mask) for value in one) for one in sets]
        order = order + [s ^ mask for s in order]
        mask //= 2
    sets[0] = (local,) + sets[0][1:]
    sets = [sets[order.index(s)] for s in range(blocks)]

    own, other = pl.pallas_call(
        functools.partial(coef_kernel, blocks=blocks),
        in_specs=smem_specs(1) + vmem_specs(5 * blocks),
        out_specs=vmem_specs(2),
        out_shape=[
            pltpu.VMEM((half + EXTRA, LANES), jnp.bfloat16),
            pltpu.VMEM((half, LANES), jnp.bfloat16),
        ],
        scratch_shapes=[
            pltpu.VMEM((blocks, 8, LANES), jnp.float32),
            pltpu.VMEM((blocks, 3, LANES), jnp.float32),
        ],
        compiler_params=pltpu.CompilerParams(vmem_limit_bytes=VMEM_LIMIT),
        name="coefficients",
    )(me, *[resident(one[n]) for n in range(5) for one in sets])

    def morph(total, chunks, last):
        count = len(chunks)
        first = total is None
        operands = [feats] + ([] if first else [total])
        operands += [chunk[0] for chunk in chunks] + [chunk[1] for chunk in chunks]
        work = node_count * count * 2 * half
        scratch = [pltpu.VMEM((DEPTH, 2 * half * count), jnp.bfloat16)]
        if last:
            scratch += [
                pltpu.VMEM((node_count, LANES), jnp.float32),
                pltpu.SemaphoreType.DMA((node_count // tile,)),
            ]
        out = jax.ShapeDtypeStruct if last else pltpu.VMEM
        return pl.pallas_call(
            functools.partial(
                morph_kernel, blocks=blocks, chunks=count, first=first, last=last, tile=tile
            ),
            in_specs=vmem_specs(len(operands)),
            out_specs=pl.BlockSpec(memory_space=pl.ANY) if last else vmem_specs(1)[0],
            out_shape=out((node_count, LANES), jnp.float32),
            scratch_shapes=scratch,
            input_output_aliases={} if first or last else {1: 0},
            cost_estimate=pl.CostEstimate(
                flops=work * 600, transcendentals=work, bytes_accessed=node_count * LANES * 8
            ),
            compiler_params=pltpu.CompilerParams(vmem_limit_bytes=VMEM_LIMIT),
        name="morph",
        )(*[resident(value) for value in operands])

    total = None
    chunks = [(own, other)]
    fresh = chunks
    mask = columns // 2
    while mask:
        arrived = [swap(chunk[0], "nodes", columns, mask) for chunk in chunks]
        total = morph(total, fresh, False)
        fresh = [(value, swap(value, "cblk", blocks, 1)) for value in arrived]
        chunks = chunks + fresh
        mask //= 2
    return morph(total, fresh, True)


def solution(mesh):
    placed = (
        P(("nodes", "cblk"), None),
        P(("nodes", "cblk"), None),
        P(("nodes", "cblk")),
        P(("nodes", "cblk")),
        P(None, ("nodes", "cblk")),
        P(None, ("nodes", "cblk")),
        P(("nodes", "cblk"), None),
    )
    return jax.shard_map(
        per_device,
        mesh=mesh,
        in_specs=placed,
        out_specs=P(("nodes", "cblk"), None),
        check_vma=False,
    )
```

```python
import functools

import jax
import jax.numpy as jnp
from jax import lax
from jax.experimental import pallas as pl
from jax.experimental.pallas import tpu as pltpu
from jax.sharding import PartitionSpec as P

LANES = 128
EXTRA = 16
DEPTH = 32
FAR = 64.0
VMEM_LIMIT = 24 * 1024 * 1024
MOST = 4
SUPPORT_RADIUS = 0.3
GAIN = 16.0 / (SUPPORT_RADIUS * SUPPORT_RADIUS)


def split3(value):
    high = value.astype(jnp.bfloat16).astype(jnp.float32)
    rest = value - high
    middle = rest.astype(jnp.bfloat16).astype(jnp.float32)
    return high, middle, rest - middle


def stack_rows(rows, width):
    rows = rows + [jnp.zeros((1, width), jnp.float32)] * (DEPTH - len(rows))
    return jnp.concatenate(rows, axis=0).astype(jnp.bfloat16)


def pack_kernel(sens_ref, owner_ref, slot_ref, scale_ref, pos_ref, out_ref):
    row_count = sens_ref.shape[0]
    out_ref[0:row_count, :] = sens_ref[...]
    rows = [pos_ref[...].astype(jnp.float32)] + list(split3(scale_ref[...]))
    rows += [owner_ref[...].astype(jnp.float32), slot_ref[...].astype(jnp.float32)]
    spare = out_ref.shape[0] - row_count - 6 - 2 * owner_ref.shape[0]
    rows.append(jnp.zeros((spare, LANES), jnp.float32))
    out_ref[row_count:, :] = jnp.concatenate(rows, axis=0).astype(jnp.bfloat16)


def feature_kernel(me_ref, support_ref, pos_ref, out_ref, *, blocks):
    count = pos_ref.shape[1]
    tiles = support_ref.shape[0]
    width = count // tiles
    core = me_ref[0] & 1
    for tile in range(tiles):
        cols = pl.ds(tile * width, width)
        points = [pos_ref[k : k + 1, cols].astype(jnp.float32) for k in range(3)]
        norm = GAIN * (points[0] * points[0] + points[1] * points[1] + points[2] * points[2])
        ones = jnp.ones_like(norm)
        rows = points * 3 + list(split3(norm)) + [ones] * 3
        for k in range(blocks):
            place = lax.rem(core * (blocks // 2) + k, blocks)
            off = (1 - support_ref[tile, place]).astype(jnp.float32)
            rows.append(ones * off)
        out_ref[cols, :] = jnp.swapaxes(stack_rows(rows, width), 0, 1)


def coef_kernel(me_ref, *refs, blocks, groups):
    packs = refs[:blocks]
    own_ref, other_ref, metas = refs[blocks:]
    me = me_ref[0]
    core = me & 1
    half = blocks // 2 * LANES
    row_count = groups * LANES
    place = lax.broadcasted_iota(jnp.int32, (blocks * LANES, LANES), 0) + core * half
    place = (place & (blocks * LANES - 1)).astype(jnp.float32)
    sums = jnp.zeros((blocks * LANES, LANES), jnp.float32)
    for s in range(blocks):
        meta = packs[s][row_count:, :].astype(jnp.float32)
        metas[s] = meta
        target = meta[6 : 6 + groups, :] * LANES + meta[6 + groups : 6 + 2 * groups, :]
        picked = jnp.concatenate(
            [
                (place == target[g : g + 1, :]).astype(jnp.float32).astype(jnp.bfloat16)
                for g in range(groups)
            ],
            axis=1,
        )
        rows = packs[s][0:row_count, :]
        sums = sums + jnp.dot(picked, rows, preferred_element_type=jnp.float32)
    pos_rows = []
    for k in range(blocks):
        meta = metas[lax.rem(core * (blocks // 2) + k, blocks) ^ me]
        scale = meta[3:4, :] + meta[4:5, :] + meta[5:6, :]
        scale = jnp.swapaxes(jnp.broadcast_to(scale, (8, LANES)), 0, 1)[:, 0:1]
        coef = (scale * sums[k * LANES : (k + 1) * LANES, :]).astype(jnp.bfloat16)
        if k < blocks // 2:
            own_ref[k * LANES : (k + 1) * LANES, :] = coef
        else:
            other_ref[k * LANES - half : (k + 1) * LANES - half, :] = coef
        pos_rows.append(meta[0:3, :])
    pos_rows.append(jnp.zeros((EXTRA - 3 * blocks, LANES), jnp.float32))
    own_ref[half : half + EXTRA, :] = jnp.concatenate(pos_rows, axis=0).astype(jnp.bfloat16)


def centre_features(chunk_ref, half, blocks, out_ref, col):
    for k in range(blocks):
        pos = chunk_ref[half : half + EXTRA, :].astype(jnp.float32)[3 * k : 3 * k + 3, :]
        axes = [pos[d : d + 1, :] for d in range(3)]
        norm = GAIN * (axes[0] * axes[0] + axes[1] * axes[1] + axes[2] * axes[2])
        parts = [split3(-2.0 * GAIN * axis) for axis in axes]
        ones = jnp.ones_like(norm)
        rows = [parts[d][p] for p in range(3) for d in range(3)] + [ones] * 3 + list(split3(norm))
        rows += [ones * (FAR if k == b else 0.0) for b in range(blocks)]
        out_ref[:, col + k * LANES : col + (k + 1) * LANES] = stack_rows(rows, LANES)


def morph_kernel(*refs, blocks, chunks, first, last, tile):
    feats_ref = refs[0]
    refs = refs[1:]
    if not first:
        acc_ref, refs = refs[0], refs[1:]
    own_refs, other_refs = refs[:chunks], refs[chunks : 2 * chunks]
    out_ref, cen_ref, coef_ref = refs[2 * chunks : 2 * chunks + 3]
    squares, weights = refs[2 * chunks + 3 : 2 * chunks + 5], refs[2 * chunks + 5 : 2 * chunks + 7]
    if last:
        done_ref, sems = refs[2 * chunks + 7 :]
    half = blocks // 2 * LANES
    for t in range(chunks):
        for h, value in enumerate((own_refs[t], other_refs[t])):
            start = 2 * half * t + half * h
            coef_ref[start : start + half, :] = value[0:half, :]
        centre_features(own_refs[t], half, blocks, cen_ref, 2 * half * t)
    steps = feats_ref.shape[0] // tile
    pieces = 2 * chunks

    def rows_of(index):
        return pl.ds(pl.multiple_of(index * tile, tile), tile)

    def measure(index, slot):
        feats = feats_ref[rows_of(index), :]
        for p in range(pieces):
            cols = slice(p * half, (p + 1) * half)
            squares[slot][:, cols] = jnp.dot(
                feats, cen_ref[:, cols], preferred_element_type=jnp.float32
            )

    def weigh(slot):
        for p in range(pieces):
            cols = slice(p * half, (p + 1) * half)
            square = jnp.maximum(squares[slot][:, cols], 1e-30)
            reach = square * lax.rsqrt(square)
            base = jnp.maximum(4.0 - reach, 0.0)
            base = base * base
            weights[slot][:, cols] = (base * base * (reach + 1.0)).astype(jnp.bfloat16)

    def leave(index):
        rows = rows_of(index)
        return pltpu.make_async_copy(done_ref.at[rows, :], out_ref.at[rows, :], sems.at[index])

    def gather(index, slot):
        rows = rows_of(index)
        total = jnp.dot(weights[slot][...], coef_ref[...], preferred_element_type=jnp.float32)
        if not first:
            total = acc_ref[rows, :] + total
        if last:
            done_ref[rows, :] = total * (1.0 / 256.0)
        else:
            out_ref[rows, :] = total

    def pair(index, carry):
        even = 2 * index
        weigh(1)
        measure(even + 2, 0)
        gather(even, 0)
        weigh(0)
        measure(even + 3, 1)
        gather(even + 1, 1)
        if last:
            leave(even).start()
            leave(even + 1).start()
        return carry

    measure(0, 0)
    weigh(0)
    measure(1, 1)
    lax.fori_loop(0, steps // 2 - 1, pair, 0)
    weigh(1)
    gather(steps - 2, 0)
    gather(steps - 1, 1)
    if last:
        leave(steps - 2).start()
        leave(steps - 1).start()

        def settle(index, carry):
            leave(index).wait()
            return carry

        lax.fori_loop(0, steps, settle, 0)


def vmem_specs(count):
    return [pl.BlockSpec(memory_space=pltpu.VMEM) for _ in range(count)]


def resident(value):
    return pltpu.with_memory_space_constraint(value, pltpu.VMEM)


def smem_specs(count):
    return [pl.BlockSpec(memory_space=pltpu.SMEM) for _ in range(count)]


def per_device(sens, dest_owner, dest_slot, coef_scale, centre_pos, node_pos, support):
    blocks = lax.axis_size("cblk")
    columns = lax.axis_size("nodes")
    row_count = sens.shape[0]
    groups = row_count // LANES
    half = blocks // 2 * LANES
    node_count = node_pos.shape[1]
    tile = 256
    me = lax.axis_index("cblk").astype(jnp.int32)[None]

    def swap(value, axis, size, mask):
        return lax.ppermute(value, axis, [(i, i ^ mask) for i in range(size)])

    params = pltpu.CompilerParams(vmem_limit_bytes=VMEM_LIMIT)
    extra = -(-(6 + 2 * groups) // EXTRA) * EXTRA
    pack = pl.pallas_call(
        pack_kernel,
        in_specs=vmem_specs(5),
        out_specs=vmem_specs(1)[0],
        out_shape=pltpu.VMEM((row_count + extra, LANES), jnp.bfloat16),
        compiler_params=params,
        name="pack",
    )(
        sens,
        dest_owner.reshape(groups, LANES),
        dest_slot.reshape(groups, LANES),
        coef_scale.reshape(1, LANES),
        centre_pos,
    )
    packs, order = [pack], [0]
    mask = blocks // 2
    while mask:
        packs = packs + [swap(value, "cblk", blocks, mask) for value in packs]
        order = order + [s ^ mask for s in order]
        mask //= 2
    packs = [packs[order.index(s)] for s in range(blocks)]

    feats = pl.pallas_call(
        functools.partial(feature_kernel, blocks=blocks),
        in_specs=smem_specs(2) + vmem_specs(1),
        out_specs=vmem_specs(1)[0],
        out_shape=pltpu.VMEM((node_count, DEPTH), jnp.bfloat16),
        compiler_params=params,
        cost_estimate=pl.CostEstimate(
            flops=node_count * 10000, transcendentals=0, bytes_accessed=node_count * 8
        ),
        name="features",
    )(me, support, node_pos)

    own, other = pl.pallas_call(
        functools.partial(coef_kernel, blocks=blocks, groups=groups),
        in_specs=smem_specs(1) + vmem_specs(blocks),
        out_specs=vmem_specs(2),
        out_shape=[
            pltpu.VMEM((half + EXTRA, LANES), jnp.bfloat16),
            pltpu.VMEM((half, LANES), jnp.bfloat16),
        ],
        scratch_shapes=[pltpu.VMEM((blocks, extra, LANES), jnp.float32)],
        compiler_params=params,
        name="coefficients",
    )(me, *[resident(value) for value in packs])

    def morph_call(total, chunks, last):
        count = len(chunks)
        first = total is None
        operands = [feats] + ([] if first else [total])
        operands += [chunk[0] for chunk in chunks] + [chunk[1] for chunk in chunks]
        width = 2 * half * count
        work = node_count * width
        scratch = [pltpu.VMEM((DEPTH, width), jnp.bfloat16), pltpu.VMEM((width, LANES), jnp.bfloat16)]
        scratch += [pltpu.VMEM((tile, width), jnp.float32)] * 2
        scratch += [pltpu.VMEM((tile, width), jnp.bfloat16)] * 2
        if last:
            scratch += [
                pltpu.VMEM((node_count, LANES), jnp.float32),
                pltpu.SemaphoreType.DMA((node_count // tile,)),
            ]
        out = jax.ShapeDtypeStruct if last else pltpu.VMEM
        return pl.pallas_call(
            functools.partial(
                morph_kernel, blocks=blocks, chunks=count, first=first, last=last, tile=tile
            ),
            in_specs=vmem_specs(len(operands)),
            out_specs=pl.BlockSpec(memory_space=pl.ANY) if last else vmem_specs(1)[0],
            out_shape=out((node_count, LANES), jnp.float32),
            scratch_shapes=scratch,
            input_output_aliases={} if first or last else {1: 0},
            cost_estimate=pl.CostEstimate(
                flops=work * 600, transcendentals=work, bytes_accessed=node_count * LANES * 8
            ),
            compiler_params=params,
            name="morph",
        )(*[resident(value) for value in operands])

    def morph(total, chunks, last=False):
        for start in range(0, len(chunks), MOST):
            done = start + MOST >= len(chunks)
            total = morph_call(total, chunks[start : start + MOST], last and done)
        return total

    def node_swap(value, mask):
        return swap(value, "nodes", columns, mask)

    def with_other(values):
        return [(value, swap(value, "cblk", blocks, 1)) for value in values]

    total = None
    have, fresh, ready = [own], [own], [(own, other)]
    mask = columns // 2
    while mask > 1:
        arrived = [node_swap(value, mask) for value in have]
        early = [node_swap(value, 1) for value in fresh]
        total = morph(total, ready)
        have, arrived, early, total = lax.optimization_barrier((have, arrived, early, total))
        have, fresh = have + arrived, arrived
        ready = with_other(arrived + early)
        mask //= 2
    late = [node_swap(value, 1) for value in fresh]
    total = morph(total, ready)
    late, total = lax.optimization_barrier((late, total))
    return morph(total, with_other(late), True)


def solution(mesh):
    placed = (
        P(("nodes", "cblk"), None),
        P(("nodes", "cblk"), None),
        P(("nodes", "cblk")),
        P(("nodes", "cblk")),
        P(None, ("nodes", "cblk")),
        P(None, ("nodes", "cblk")),
        P(("nodes", "cblk"), None),
    )
    return jax.shard_map(
        per_device,
        mesh=mesh,
        in_specs=placed,
        out_specs=P(("nodes", "cblk"), None),
        check_vma=False,
    )
```

```python
import functools

import jax
import jax.numpy as jnp
from jax import lax
from jax.experimental import pallas as pl
from jax.experimental.pallas import tpu as pltpu
from jax.sharding import PartitionSpec as P

LANES = 128
EXTRA = 16
DEPTH = 32
FAR = 64.0
VMEM_LIMIT = 24 * 1024 * 1024
UNROLLED = 4
SUPPORT_RADIUS = 0.3
GAIN = 16.0 / (SUPPORT_RADIUS * SUPPORT_RADIUS)


def split3(value):
    high = value.astype(jnp.bfloat16).astype(jnp.float32)
    rest = value - high
    middle = rest.astype(jnp.bfloat16).astype(jnp.float32)
    return high, middle, rest - middle


def stack_rows(rows, width):
    rows = rows + [jnp.zeros((1, width), jnp.float32)] * (DEPTH - len(rows))
    return jnp.concatenate(rows, axis=0).astype(jnp.bfloat16)


def pack_kernel(*refs):
    sources, out_ref, targets, sems = refs[:5], refs[5], refs[6:10], refs[10]
    row_count = sources[0].shape[0]
    targets = (out_ref.at[pl.ds(0, row_count), :],) + targets
    copies = [
        pltpu.make_async_copy(source, target, sems.at[n])
        for n, (source, target) in enumerate(zip(sources, targets))
    ]
    for copy in copies:
        copy.start()
    for copy in copies[1:]:
        copy.wait()
    owner, slot, scale, pos = (target[...] for target in targets[1:])
    rows = [pos.astype(jnp.float32)] + list(split3(scale))
    rows += [owner.astype(jnp.float32), slot.astype(jnp.float32)]
    spare = out_ref.shape[0] - row_count - 6 - 2 * owner.shape[0]
    rows.append(jnp.zeros((spare, LANES), jnp.float32))
    out_ref[row_count:, :] = jnp.concatenate(rows, axis=0).astype(jnp.bfloat16)
    copies[0].wait()


def join_kernel(*refs):
    start = 0
    for ref in refs[:-1]:
        refs[-1][start : start + ref.shape[0], :] = ref[...]
        start += ref.shape[0]


def feature_kernel(me_ref, support_ref, pos_ref, out_ref, *, blocks):
    count = pos_ref.shape[1]
    tiles = support_ref.shape[0]
    width = count // tiles
    core = me_ref[0] & 1
    for tile in range(tiles):
        cols = pl.ds(tile * width, width)
        points = [pos_ref[k : k + 1, cols].astype(jnp.float32) for k in range(3)]
        norm = GAIN * (points[0] * points[0] + points[1] * points[1] + points[2] * points[2])
        ones = jnp.ones_like(norm)
        rows = points * 3 + list(split3(norm)) + [ones] * 3
        for k in range(blocks):
            place = lax.rem(core * (blocks // 2) + k, blocks)
            off = (1 - support_ref[tile, place]).astype(jnp.float32)
            rows.append(ones * off)
        out_ref[cols, :] = jnp.swapaxes(stack_rows(rows, width), 0, 1)


def coef_kernel(me_ref, *refs, blocks, groups):
    packs = refs[:blocks]
    own_ref, other_ref, metas = refs[blocks:]
    me = me_ref[0]
    core = me & 1
    half = blocks // 2 * LANES
    row_count = groups * LANES
    place = lax.broadcasted_iota(jnp.int32, (blocks * LANES, LANES), 0) + core * half
    place = (place & (blocks * LANES - 1)).astype(jnp.float32)
    sums = jnp.zeros((blocks * LANES, LANES), jnp.float32)
    for s in range(blocks):
        meta = packs[s][row_count:, :].astype(jnp.float32)
        metas[s] = meta
        target = meta[6 : 6 + groups, :] * LANES + meta[6 + groups : 6 + 2 * groups, :]
        picked = jnp.concatenate(
            [
                (place == target[g : g + 1, :]).astype(jnp.float32).astype(jnp.bfloat16)
                for g in range(groups)
            ],
            axis=1,
        )
        rows = packs[s][0:row_count, :]
        sums = sums + jnp.dot(picked, rows, preferred_element_type=jnp.float32)
    pos_rows = []
    for k in range(blocks):
        meta = metas[lax.rem(core * (blocks // 2) + k, blocks) ^ me]
        scale = meta[3:4, :] + meta[4:5, :] + meta[5:6, :]
        scale = jnp.swapaxes(jnp.broadcast_to(scale, (8, LANES)), 0, 1)[:, 0:1]
        coef = (scale * sums[k * LANES : (k + 1) * LANES, :]).astype(jnp.bfloat16)
        if k < blocks // 2:
            own_ref[k * LANES : (k + 1) * LANES, :] = coef
        else:
            other_ref[k * LANES - half : (k + 1) * LANES - half, :] = coef
        pos_rows.append(meta[0:3, :])
    pos_rows.append(jnp.zeros((EXTRA - 3 * blocks, LANES), jnp.float32))
    own_ref[half : half + EXTRA, :] = jnp.concatenate(pos_rows, axis=0).astype(jnp.bfloat16)


def centre_features(chunk_ref, row, blocks, out_ref, col):
    points = chunk_ref[row : row + EXTRA, :].astype(jnp.float32)
    for k in range(blocks):
        pos = points[3 * k : 3 * k + 3, :]
        axes = [pos[d : d + 1, :] for d in range(3)]
        norm = GAIN * (axes[0] * axes[0] + axes[1] * axes[1] + axes[2] * axes[2])
        parts = [split3(-2.0 * GAIN * axis) for axis in axes]
        ones = jnp.ones_like(norm)
        rows = [parts[d][p] for p in range(3) for d in range(3)] + [ones] * 3 + list(split3(norm))
        rows += [ones * (FAR if k == b else 0.0) for b in range(blocks)]
        out_ref[:, col + k * LANES : col + (k + 1) * LANES] = stack_rows(rows, LANES)


def morph_kernel(*refs, blocks, counts, first, last, tile):
    feats_ref = refs[0]
    refs = refs[1:]
    if not first:
        acc_ref, refs = refs[0], refs[1:]
    arrays = len(counts)
    own_refs, other_refs = refs[:arrays], refs[arrays : 2 * arrays]
    out_ref, cen_ref, coef_ref = refs[2 * arrays : 2 * arrays + 3]
    if last:
        done_ref, sems = refs[2 * arrays + 3 :]
    half = blocks // 2 * LANES
    stride = half + EXTRA
    start = 0
    for t in range(arrays):
        for n in range(counts[t]):
            centre_features(own_refs[t], n * stride + half, blocks, cen_ref, start)
            for value in (own_refs[t], other_refs[t]):
                rows = slice(start, start + half)
                coef_ref[rows, 0:LANES] = value[n * stride : n * stride + half, :]
                coef_ref[rows, LANES:] = jnp.zeros((half, LANES), jnp.bfloat16)
                start += half
    steps = feats_ref.shape[0] // tile

    def rows_of(index):
        return pl.ds(index * tile if unrolled else pl.multiple_of(index * tile, tile), tile)

    def leave(index):
        rows = rows_of(index)
        return pltpu.make_async_copy(done_ref.at[rows, :], out_ref.at[rows, :], sems.at[index])

    def settle(index, carry):
        leave(index).wait()
        return carry

    def step(index, carry):
        rows = rows_of(index)
        feats = feats_ref[rows, :]
        total = None if first else acc_ref[rows, :]
        for piece in range(start // half):
            cols = slice(piece * half, (piece + 1) * half)
            square = jnp.dot(feats, cen_ref[:, cols], preferred_element_type=jnp.float32)
            square = jnp.maximum(square, 1e-30)
            reach = square * lax.rsqrt(square)
            base = jnp.maximum(4.0 - reach, 0.0)
            base = base * base
            weight = (base * base * (reach + 1.0)).astype(jnp.bfloat16)
            part = jnp.dot(weight, coef_ref[cols, :], preferred_element_type=jnp.float32)
            part = part[:, 0:LANES]
            total = part if total is None else total + part
        if last:
            done_ref[rows, :] = total * (1.0 / 256.0)
            leave(index).start()
        else:
            out_ref[rows, :] = total
        return carry

    def over_tiles(body):
        if unrolled:
            for index in range(steps):
                body(index, 0)
        else:
            lax.fori_loop(0, steps, body, 0)

    unrolled = sum(counts) <= UNROLLED
    over_tiles(step)
    if last:
        over_tiles(settle)


def vmem_specs(count):
    return [pl.BlockSpec(memory_space=pltpu.VMEM) for _ in range(count)]


def resident(value):
    return pltpu.with_memory_space_constraint(value, pltpu.VMEM)


def smem_specs(count):
    return [pl.BlockSpec(memory_space=pltpu.SMEM) for _ in range(count)]


def per_device(sens, dest_owner, dest_slot, coef_scale, centre_pos, node_pos, support):
    blocks = lax.axis_size("cblk")
    columns = lax.axis_size("nodes")
    row_count = sens.shape[0]
    groups = row_count // LANES
    half = blocks // 2 * LANES
    node_count = node_pos.shape[1]
    tile = 128
    me = lax.axis_index("cblk").astype(jnp.int32)[None]

    def swap(value, axis, size, mask):
        return lax.ppermute(value, axis, [(i, i ^ mask) for i in range(size)])

    params = pltpu.CompilerParams(vmem_limit_bytes=VMEM_LIMIT)
    extra = -(-(6 + 2 * groups) // EXTRA) * EXTRA
    pack = pl.pallas_call(
        pack_kernel,
        in_specs=[pl.BlockSpec(memory_space=pl.ANY)] * 5,
        out_specs=vmem_specs(1)[0],
        out_shape=pltpu.VMEM((row_count + extra, LANES), jnp.bfloat16),
        scratch_shapes=[
            pltpu.VMEM((groups, LANES), jnp.int32),
            pltpu.VMEM((groups, LANES), jnp.int32),
            pltpu.VMEM((1, LANES), jnp.float32),
            pltpu.VMEM(centre_pos.shape, jnp.bfloat16),
            pltpu.SemaphoreType.DMA((5,)),
        ],
        compiler_params=params,
        name="pack",
    )(
        *[
            pltpu.with_memory_space_constraint(value, pltpu.HBM)
            for value in (
                sens,
                dest_owner.reshape(groups, LANES),
                dest_slot.reshape(groups, LANES),
                coef_scale.reshape(1, LANES),
                centre_pos,
            )
        ]
    )
    feats = pl.pallas_call(
        functools.partial(feature_kernel, blocks=blocks),
        in_specs=smem_specs(2) + vmem_specs(1),
        out_specs=vmem_specs(1)[0],
        out_shape=pltpu.VMEM((node_count, DEPTH), jnp.bfloat16),
        compiler_params=params,
        cost_estimate=pl.CostEstimate(
            flops=node_count * 10000, transcendentals=0, bytes_accessed=node_count * 8
        ),
        name="features",
    )(me, support, node_pos)

    packs, order = [pack], [0]
    mask = blocks // 2
    while mask:
        arrived = [swap(value, "cblk", blocks, mask) for value in packs]
        if mask == blocks // 2:
            arrived, feats = lax.optimization_barrier((arrived, feats))
        packs = packs + arrived
        order = order + [s ^ mask for s in order]
        mask //= 2
    packs = [packs[order.index(s)] for s in range(blocks)]

    own, other = pl.pallas_call(
        functools.partial(coef_kernel, blocks=blocks, groups=groups),
        in_specs=smem_specs(1) + vmem_specs(blocks),
        out_specs=vmem_specs(2),
        out_shape=[
            pltpu.VMEM((half + EXTRA, LANES), jnp.bfloat16),
            pltpu.VMEM((half, LANES), jnp.bfloat16),
        ],
        scratch_shapes=[pltpu.VMEM((blocks, extra, LANES), jnp.float32)],
        compiler_params=params,
        name="coefficients",
    )(me, *[resident(value) for value in packs])

    stride = half + EXTRA

    def count_of(value):
        return value.shape[0] // stride

    def join(values):
        return pl.pallas_call(
            join_kernel,
            in_specs=vmem_specs(len(values)),
            out_specs=vmem_specs(1)[0],
            out_shape=pltpu.VMEM((stride * sum(count_of(v) for v in values), LANES), jnp.bfloat16),
            compiler_params=params,
            name="join",
        )(*[resident(value) for value in values])

    def morph(total, pairs, last=False):
        counts = tuple(count_of(pair[0]) for pair in pairs)
        first = total is None
        operands = [feats] + ([] if first else [total])
        operands += [pair[0] for pair in pairs] + [pair[1] for pair in pairs]
        width = 2 * half * sum(counts)
        work = node_count * width
        scratch = [
            pltpu.VMEM((DEPTH, width), jnp.bfloat16),
            pltpu.VMEM((width, 2 * LANES), jnp.bfloat16),
        ]
        if last:
            scratch += [
                pltpu.VMEM((node_count, LANES), jnp.float32),
                pltpu.SemaphoreType.DMA((node_count // tile,)),
            ]
        out = jax.ShapeDtypeStruct if last else pltpu.VMEM
        return pl.pallas_call(
            functools.partial(
                morph_kernel, blocks=blocks, counts=counts, first=first, last=last, tile=tile
            ),
            in_specs=vmem_specs(len(operands)),
            out_specs=pl.BlockSpec(memory_space=pl.ANY) if last else vmem_specs(1)[0],
            out_shape=out((node_count, LANES), jnp.float32),
            scratch_shapes=scratch,
            input_output_aliases={} if first or last else {1: 0},
            cost_estimate=pl.CostEstimate(
                flops=work * 600, transcendentals=work, bytes_accessed=node_count * LANES * 8
            ),
            compiler_params=pltpu.CompilerParams(
                vmem_limit_bytes=VMEM_LIMIT
            ),
            name="morph",
        )(*[resident(value) for value in operands])

    def node_swap(value, mask):
        return swap(value, "nodes", columns, mask)

    def with_other(values):
        return [(value, swap(value, "cblk", blocks, 1)) for value in values]

    total, mask = None, columns // 2
    have, ready, early = own, [(own, other)], []
    while mask > 1:
        arrived = node_swap(have, mask)
        if mask == 2:
            early = [node_swap(have, 1)]
        total = morph(total, ready)
        have, arrived, early, total = lax.optimization_barrier((have, arrived, early, total))
        ready = with_other([arrived] + early)
        if mask > 2:
            have = join([have, arrived])
        mask //= 2
    late = node_swap(arrived, 1)
    total = morph(total, ready)
    late, total = lax.optimization_barrier((late, total))
    return morph(total, with_other([late]), True)


def solution(mesh):
    placed = (
        P(("nodes", "cblk"), None),
        P(("nodes", "cblk"), None),
        P(("nodes", "cblk")),
        P(("nodes", "cblk")),
        P(None, ("nodes", "cblk")),
        P(None, ("nodes", "cblk")),
        P(("nodes", "cblk"), None),
    )
    return jax.shard_map(
        per_device,
        mesh=mesh,
        in_specs=placed,
        out_specs=P(("nodes", "cblk"), None),
        check_vma=False,
    )
```

```python
import functools

import jax
import jax.numpy as jnp
from jax import lax
from jax.experimental import pallas as pl
from jax.experimental.pallas import tpu as pltpu
from jax.sharding import PartitionSpec as P

LANES = 128
EXTRA = 16
DEPTH = 32
FAR = 64.0
VMEM_LIMIT = 24 * 1024 * 1024
UNROLLED = 4
SUPPORT_RADIUS = 0.3
GAIN = 16.0 / (SUPPORT_RADIUS * SUPPORT_RADIUS)


def split3(value):
    high = value.astype(jnp.bfloat16).astype(jnp.float32)
    rest = value - high
    middle = rest.astype(jnp.bfloat16).astype(jnp.float32)
    return high, middle, rest - middle


def stack_rows(rows, width):
    rows = rows + [jnp.zeros((1, width), jnp.float32)] * (DEPTH - len(rows))
    return jnp.concatenate(rows, axis=0).astype(jnp.bfloat16)


def pack_kernel(*refs):
    sources, out_ref, targets, sems = refs[:5], refs[5], refs[6:10], refs[10]
    row_count = sources[0].shape[0]
    targets = (out_ref.at[pl.ds(0, row_count), :],) + targets
    copies = [
        pltpu.make_async_copy(source, target, sems.at[n])
        for n, (source, target) in enumerate(zip(sources, targets))
    ]
    for copy in copies:
        copy.start()
    for copy in copies[1:]:
        copy.wait()
    owner, slot, scale, pos = (target[...] for target in targets[1:])
    rows = [pos.astype(jnp.float32)] + list(split3(scale))
    rows += [owner.astype(jnp.float32), slot.astype(jnp.float32)]
    spare = out_ref.shape[0] - row_count - 6 - 2 * owner.shape[0]
    rows.append(jnp.zeros((spare, LANES), jnp.float32))
    out_ref[row_count:, :] = jnp.concatenate(rows, axis=0).astype(jnp.bfloat16)
    copies[0].wait()


def join_kernel(*refs):
    start = 0
    for ref in refs[:-1]:
        refs[-1][start : start + ref.shape[0], :] = ref[...]
        start += ref.shape[0]


def feature_kernel(me_ref, support_ref, pos_ref, out_ref, *, blocks):
    count = pos_ref.shape[1]
    tiles = support_ref.shape[0]
    width = count // tiles
    core = me_ref[0] & 1
    for tile in range(tiles):
        cols = pl.ds(tile * width, width)
        points = [pos_ref[k : k + 1, cols].astype(jnp.float32) for k in range(3)]
        norm = GAIN * (points[0] * points[0] + points[1] * points[1] + points[2] * points[2])
        ones = jnp.ones_like(norm)
        rows = points * 3 + list(split3(norm)) + [ones] * 3
        for k in range(blocks):
            place = lax.rem(core * (blocks // 2) + k, blocks)
            off = (1 - support_ref[tile, place]).astype(jnp.float32)
            rows.append(ones * off)
        out_ref[cols, :] = jnp.swapaxes(stack_rows(rows, width), 0, 1)


def coef_kernel(me_ref, *refs, blocks, groups):
    packs = refs[:blocks]
    own_ref, other_ref, metas = refs[blocks:]
    me = me_ref[0]
    core = me & 1
    half = blocks // 2 * LANES
    row_count = groups * LANES
    place = lax.broadcasted_iota(jnp.int32, (blocks * LANES, LANES), 0) + core * half
    place = (place & (blocks * LANES - 1)).astype(jnp.float32)
    sums = jnp.zeros((blocks * LANES, LANES), jnp.float32)
    for s in range(blocks):
        meta = packs[s][row_count:, :].astype(jnp.float32)
        metas[s] = meta
        target = meta[6 : 6 + groups, :] * LANES + meta[6 + groups : 6 + 2 * groups, :]
        picked = jnp.concatenate(
            [
                (place == target[g : g + 1, :]).astype(jnp.float32).astype(jnp.bfloat16)
                for g in range(groups)
            ],
            axis=1,
        )
        rows = packs[s][0:row_count, :]
        sums = sums + jnp.dot(picked, rows, preferred_element_type=jnp.float32)
    pos_rows = []
    for k in range(blocks):
        meta = metas[lax.rem(core * (blocks // 2) + k, blocks) ^ me]
        scale = meta[3:4, :] + meta[4:5, :] + meta[5:6, :]
        scale = jnp.swapaxes(jnp.broadcast_to(scale, (8, LANES)), 0, 1)[:, 0:1]
        coef = (scale * sums[k * LANES : (k + 1) * LANES, :]).astype(jnp.bfloat16)
        if k < blocks // 2:
            own_ref[k * LANES : (k + 1) * LANES, :] = coef
        else:
            other_ref[k * LANES - half : (k + 1) * LANES - half, :] = coef
        pos_rows.append(meta[0:3, :])
    pos_rows.append(jnp.zeros((EXTRA - 3 * blocks, LANES), jnp.float32))
    own_ref[half : half + EXTRA, :] = jnp.concatenate(pos_rows, axis=0).astype(jnp.bfloat16)


def centre_features(chunk_ref, row, side, blocks, out_ref, col):
    points = chunk_ref[row : row + EXTRA, :].astype(jnp.float32)
    for n in range(blocks // 2):
        k = side * (blocks // 2) + n
        pos = points[3 * k : 3 * k + 3, :]
        axes = [pos[d : d + 1, :] for d in range(3)]
        norm = GAIN * (axes[0] * axes[0] + axes[1] * axes[1] + axes[2] * axes[2])
        parts = [split3(-2.0 * GAIN * axis) for axis in axes]
        ones = jnp.ones_like(norm)
        rows = [parts[d][p] for p in range(3) for d in range(3)] + [ones] * 3 + list(split3(norm))
        rows += [ones * (FAR if k == b else 0.0) for b in range(blocks)]
        out_ref[:, col + n * LANES : col + (n + 1) * LANES] = stack_rows(rows, LANES)


def morph_kernel(*refs, blocks, parts, first, last, tile):
    feats_ref = refs[0]
    refs = refs[1:]
    if not first:
        acc_ref, refs = refs[0], refs[1:]
    arrays = len(parts)
    chunk_refs, value_refs = refs[:arrays], refs[arrays : 2 * arrays]
    out_ref, cen_ref, coef_ref = refs[2 * arrays : 2 * arrays + 3]
    if last:
        done_ref, sems = refs[2 * arrays + 3 :]
    half = blocks // 2 * LANES
    stride = half + EXTRA
    start = 0
    for (count, side), chunk_ref, value_ref in zip(parts, chunk_refs, value_refs):
        for n in range(count):
            centre_features(chunk_ref, n * stride + half, side, blocks, cen_ref, start)
            rows = slice(start, start + half)
            coef_ref[rows, 0:LANES] = value_ref[n * stride : n * stride + half, :]
            coef_ref[rows, LANES:] = jnp.zeros((half, LANES), jnp.bfloat16)
            start += half
    steps = feats_ref.shape[0] // tile

    def rows_of(index):
        return pl.ds(index * tile if unrolled else pl.multiple_of(index * tile, tile), tile)

    def leave(index):
        rows = rows_of(index)
        return pltpu.make_async_copy(done_ref.at[rows, :], out_ref.at[rows, :], sems.at[index])

    def settle(index, carry):
        leave(index).wait()
        return carry

    def step(index, carry):
        rows = rows_of(index)
        feats = feats_ref[rows, :]
        total = None if first else acc_ref[rows, :]
        for piece in range(start // half):
            cols = slice(piece * half, (piece + 1) * half)
            square = jnp.dot(feats, cen_ref[:, cols], preferred_element_type=jnp.float32)
            square = jnp.maximum(square, 1e-30)
            reach = square * lax.rsqrt(square)
            base = jnp.maximum(4.0 - reach, 0.0)
            base = base * base
            weight = (base * base * (reach + 1.0)).astype(jnp.bfloat16)
            part = jnp.dot(weight, coef_ref[cols, :], preferred_element_type=jnp.float32)
            part = part[:, 0:LANES]
            total = part if total is None else total + part
        if last:
            done_ref[rows, :] = total * (1.0 / 256.0)
            leave(index).start()
        else:
            out_ref[rows, :] = total
        return carry

    def over_tiles(body):
        if unrolled:
            for index in range(steps):
                body(index, 0)
        else:
            lax.fori_loop(0, steps, body, 0)

    unrolled = start // half <= UNROLLED
    over_tiles(step)
    if last:
        over_tiles(settle)


def vmem_specs(count):
    return [pl.BlockSpec(memory_space=pltpu.VMEM) for _ in range(count)]


def resident(value):
    return pltpu.with_memory_space_constraint(value, pltpu.VMEM)


def smem_specs(count):
    return [pl.BlockSpec(memory_space=pltpu.SMEM) for _ in range(count)]


def per_device(sens, dest_owner, dest_slot, coef_scale, centre_pos, node_pos, support):
    blocks = lax.axis_size("cblk")
    columns = lax.axis_size("nodes")
    row_count = sens.shape[0]
    groups = row_count // LANES
    half = blocks // 2 * LANES
    node_count = node_pos.shape[1]
    tile = 128
    me = lax.axis_index("cblk").astype(jnp.int32)[None]

    def swap(value, axis, size, mask):
        return lax.ppermute(value, axis, [(i, i ^ mask) for i in range(size)])

    params = pltpu.CompilerParams(vmem_limit_bytes=VMEM_LIMIT)
    extra = -(-(6 + 2 * groups) // EXTRA) * EXTRA
    pack = pl.pallas_call(
        pack_kernel,
        in_specs=[pl.BlockSpec(memory_space=pl.ANY)] * 5,
        out_specs=vmem_specs(1)[0],
        out_shape=pltpu.VMEM((row_count + extra, LANES), jnp.bfloat16),
        scratch_shapes=[
            pltpu.VMEM((groups, LANES), jnp.int32),
            pltpu.VMEM((groups, LANES), jnp.int32),
            pltpu.VMEM((1, LANES), jnp.float32),
            pltpu.VMEM(centre_pos.shape, jnp.bfloat16),
            pltpu.SemaphoreType.DMA((5,)),
        ],
        compiler_params=params,
        name="pack",
    )(
        *[
            pltpu.with_memory_space_constraint(value, pltpu.HBM)
            for value in (
                sens,
                dest_owner.reshape(groups, LANES),
                dest_slot.reshape(groups, LANES),
                coef_scale.reshape(1, LANES),
                centre_pos,
            )
        ]
    )
    feats = pl.pallas_call(
        functools.partial(feature_kernel, blocks=blocks),
        in_specs=smem_specs(2) + vmem_specs(1),
        out_specs=vmem_specs(1)[0],
        out_shape=pltpu.VMEM((node_count, DEPTH), jnp.bfloat16),
        compiler_params=params,
        cost_estimate=pl.CostEstimate(
            flops=node_count * 10000, transcendentals=0, bytes_accessed=node_count * 8
        ),
        name="features",
    )(me, support, node_pos)

    packs, order = [pack], [0]
    mask = blocks // 2
    while mask:
        arrived = [swap(value, "cblk", blocks, mask) for value in packs]
        if mask == blocks // 2:
            arrived, feats = lax.optimization_barrier((arrived, feats))
        packs = packs + arrived
        order = order + [s ^ mask for s in order]
        mask //= 2
    packs = [packs[order.index(s)] for s in range(blocks)]

    own, other = pl.pallas_call(
        functools.partial(coef_kernel, blocks=blocks, groups=groups),
        in_specs=smem_specs(1) + vmem_specs(blocks),
        out_specs=vmem_specs(2),
        out_shape=[
            pltpu.VMEM((half + EXTRA, LANES), jnp.bfloat16),
            pltpu.VMEM((half, LANES), jnp.bfloat16),
        ],
        scratch_shapes=[pltpu.VMEM((blocks, extra, LANES), jnp.float32)],
        compiler_params=params,
        name="coefficients",
    )(me, *[resident(value) for value in packs])

    stride = half + EXTRA

    def count_of(value):
        return value.shape[0] // stride

    def join(values):
        return pl.pallas_call(
            join_kernel,
            in_specs=vmem_specs(len(values)),
            out_specs=vmem_specs(1)[0],
            out_shape=pltpu.VMEM((stride * sum(count_of(v) for v in values), LANES), jnp.bfloat16),
            compiler_params=params,
            name="join",
        )(*[resident(value) for value in values])

    def morph(total, pieces, last=False):
        parts = tuple((count_of(chunk), side) for chunk, _, side in pieces)
        first = total is None
        operands = [feats] + ([] if first else [total])
        operands += [chunk for chunk, _, _ in pieces] + [value for _, value, _ in pieces]
        width = half * sum(count for count, _ in parts)
        work = node_count * width
        scratch = [
            pltpu.VMEM((DEPTH, width), jnp.bfloat16),
            pltpu.VMEM((width, 2 * LANES), jnp.bfloat16),
        ]
        if last:
            scratch += [
                pltpu.VMEM((node_count, LANES), jnp.float32),
                pltpu.SemaphoreType.DMA((node_count // tile,)),
            ]
        out = jax.ShapeDtypeStruct if last else pltpu.VMEM
        return pl.pallas_call(
            functools.partial(
                morph_kernel, blocks=blocks, parts=parts, first=first, last=last, tile=tile
            ),
            in_specs=vmem_specs(len(operands)),
            out_specs=pl.BlockSpec(memory_space=pl.ANY) if last else vmem_specs(1)[0],
            out_shape=out((node_count, LANES), jnp.float32),
            scratch_shapes=scratch,
            input_output_aliases={} if first or last else {1: 0},
            cost_estimate=pl.CostEstimate(
                flops=work * 600, transcendentals=work, bytes_accessed=node_count * LANES * 8
            ),
            compiler_params=pltpu.CompilerParams(
                vmem_limit_bytes=VMEM_LIMIT
            ),
            name="morph",
        )(*[resident(value) for value in operands])

    def node_swap(value, mask):
        return swap(value, "nodes", columns, mask)

    def morph_both(total, values, last=False):
        others = [swap(value, "cblk", blocks, 1) for value in values]
        total = morph(total, [(value, value, 0) for value in values])
        return morph(total, [(value, out, 1) for value, out in zip(values, others)], last)

    mask = columns // 2
    have, ready, fresh, total = own, [], own, None
    while mask > 1:
        arrived = node_swap(have, mask)
        early = node_swap(fresh, 1)
        if total is None:
            total = morph(total, [(own, own, 0), (own, other, 1)])
        else:
            total = morph_both(total, ready)
        have, arrived, early, total = lax.optimization_barrier((have, arrived, early, total))
        ready, fresh = [arrived, early], arrived
        if mask > 2:
            have = join([have, arrived])
        mask //= 2
    late = node_swap(fresh, 1)
    total = morph_both(total, ready)
    late, total = lax.optimization_barrier((late, total))
    return morph_both(total, [late], True)


def solution(mesh):
    placed = (
        P(("nodes", "cblk"), None),
        P(("nodes", "cblk"), None),
        P(("nodes", "cblk")),
        P(("nodes", "cblk")),
        P(None, ("nodes", "cblk")),
        P(None, ("nodes", "cblk")),
        P(("nodes", "cblk"), None),
    )
    return jax.shard_map(
        per_device,
        mesh=mesh,
        in_specs=placed,
        out_specs=P(("nodes", "cblk"), None),
        check_vma=False,
    )
```

```python
import functools

import jax
import jax.numpy as jnp
from jax import lax
from jax.experimental import pallas as pl
from jax.experimental.pallas import tpu as pltpu
from jax.sharding import PartitionSpec as P


LANES = 128
EXTRA = 16
DEPTH = 32
FAR = 64.0
VMEM_LIMIT = 24 * 1024 * 1024
UNROLLED = 4
SUPPORT_RADIUS = 0.3
GAIN = 16.0 / (SUPPORT_RADIUS * SUPPORT_RADIUS)


def split3(value):
    high = value.astype(jnp.bfloat16).astype(jnp.float32)
    rest = value - high
    middle = rest.astype(jnp.bfloat16).astype(jnp.float32)
    return high, middle, rest - middle


def stack_rows(rows, width):
    rows = rows + [jnp.zeros((1, width), jnp.float32)] * (DEPTH - len(rows))
    return jnp.concatenate(rows, axis=0).astype(jnp.bfloat16)


def meta_kernel(*refs):
    sources, out_ref, targets, sems = refs[:4], refs[4], refs[5:9], refs[9]
    copies = [
        pltpu.make_async_copy(source, target, sems.at[n])
        for n, (source, target) in enumerate(zip(sources, targets))
    ]
    for copy in copies:
        copy.start()
    for copy in copies:
        copy.wait()
    owner, slot, scale, pos = (target[...] for target in targets)
    rows = [pos.astype(jnp.float32)] + list(split3(scale))
    rows += [owner.astype(jnp.float32), slot.astype(jnp.float32)]
    spare = out_ref.shape[0] - 6 - 2 * owner.shape[0]
    rows.append(jnp.zeros((spare, LANES), jnp.float32))
    out_ref[...] = jnp.concatenate(rows, axis=0).astype(jnp.bfloat16)


def join_kernel(*refs):
    start = 0
    for ref in refs[:-1]:
        refs[-1][start : start + ref.shape[0], :] = ref[...]
        start += ref.shape[0]


def feature_kernel(me_ref, support_ref, pos_ref, out_ref, *, blocks):
    count = pos_ref.shape[1]
    tiles = support_ref.shape[0]
    width = count // tiles
    core = me_ref[0] & 1
    for tile in range(tiles):
        cols = pl.ds(tile * width, width)
        points = [pos_ref[k : k + 1, cols].astype(jnp.float32) for k in range(3)]
        norm = GAIN * (points[0] * points[0] + points[1] * points[1] + points[2] * points[2])
        ones = jnp.ones_like(norm)
        rows = points * 3 + list(split3(norm)) + [ones] * 3
        for k in range(blocks):
            place = lax.rem(core * (blocks // 2) + k, blocks)
            off = (1 - support_ref[tile, place]).astype(jnp.float32)
            rows.append(ones * off)
        out_ref[cols, :] = jnp.swapaxes(stack_rows(rows, width), 0, 1)


def coef_kernel(me_ref, *refs, blocks, groups):
    rows_refs, meta_refs = refs[:blocks], refs[blocks : 2 * blocks]
    own_ref, other_ref, metas = refs[2 * blocks :]
    me = me_ref[0]
    core = me & 1
    half = blocks // 2 * LANES
    place = lax.broadcasted_iota(jnp.int32, (blocks * LANES, LANES), 0) + core * half
    place = (place & (blocks * LANES - 1)).astype(jnp.float32)
    sums = jnp.zeros((blocks * LANES, LANES), jnp.float32)
    for s in range(blocks):
        meta = meta_refs[s][...].astype(jnp.float32)
        metas[s] = meta
        target = meta[6 : 6 + groups, :] * LANES + meta[6 + groups : 6 + 2 * groups, :]
        picked = jnp.concatenate(
            [
                (place == target[g : g + 1, :]).astype(jnp.float32).astype(jnp.bfloat16)
                for g in range(groups)
            ],
            axis=1,
        )
        sums = sums + jnp.dot(picked, rows_refs[s][...], preferred_element_type=jnp.float32)
    pos_rows = []
    for k in range(blocks):
        meta = metas[lax.rem(core * (blocks // 2) + k, blocks) ^ me]
        scale = meta[3:4, :] + meta[4:5, :] + meta[5:6, :]
        scale = jnp.swapaxes(jnp.broadcast_to(scale, (8, LANES)), 0, 1)[:, 0:1]
        coef = (scale * sums[k * LANES : (k + 1) * LANES, :]).astype(jnp.bfloat16)
        if k < blocks // 2:
            own_ref[k * LANES : (k + 1) * LANES, :] = coef
        else:
            other_ref[k * LANES - half : (k + 1) * LANES - half, :] = coef
        pos_rows.append(meta[0:3, :])
    pos_rows.append(jnp.zeros((EXTRA - 3 * blocks, LANES), jnp.float32))
    own_ref[half : half + EXTRA, :] = jnp.concatenate(pos_rows, axis=0).astype(jnp.bfloat16)


def centre_features(chunk_ref, row, side, blocks, out_ref, col):
    points = chunk_ref[row : row + EXTRA, :].astype(jnp.float32)
    for n in range(blocks // 2):
        k = side * (blocks // 2) + n
        pos = points[3 * k : 3 * k + 3, :]
        axes = [pos[d : d + 1, :] for d in range(3)]
        norm = GAIN * (axes[0] * axes[0] + axes[1] * axes[1] + axes[2] * axes[2])
        parts = [split3(-2.0 * GAIN * axis) for axis in axes]
        ones = jnp.ones_like(norm)
        rows = [parts[d][p] for p in range(3) for d in range(3)] + [ones] * 3 + list(split3(norm))
        rows += [ones * (FAR if k == b else 0.0) for b in range(blocks)]
        out_ref[:, col + n * LANES : col + (n + 1) * LANES] = stack_rows(rows, LANES)


def morph_kernel(*refs, blocks, parts, first, last, tile):
    feats_ref = refs[0]
    refs = refs[1:]
    if not first:
        acc_ref, refs = refs[0], refs[1:]
    arrays = len(parts)
    chunk_refs, value_refs = refs[:arrays], refs[arrays : 2 * arrays]
    out_ref, cen_ref, coef_ref = refs[2 * arrays : 2 * arrays + 3]
    if last:
        done_ref, sems = refs[2 * arrays + 3 :]
    half = blocks // 2 * LANES
    stride = half + EXTRA
    start = 0
    for (count, side), chunk_ref, value_ref in zip(parts, chunk_refs, value_refs):
        for n in range(count):
            centre_features(chunk_ref, n * stride + half, side, blocks, cen_ref, start)
            rows = slice(start, start + half)
            coef_ref[rows, 0:LANES] = value_ref[n * stride : n * stride + half, :]
            coef_ref[rows, LANES:] = jnp.zeros((half, LANES), jnp.bfloat16)
            start += half
    steps = feats_ref.shape[0] // tile

    def rows_of(index):
        return pl.ds(index * tile if unrolled else pl.multiple_of(index * tile, tile), tile)

    def leave(index):
        rows = rows_of(index)
        return pltpu.make_async_copy(done_ref.at[rows, :], out_ref.at[rows, :], sems.at[index])

    def settle(index, carry):
        leave(index).wait()
        return carry

    def step(index, carry):
        rows = rows_of(index)
        feats = feats_ref[rows, :]
        total = None if first else acc_ref[rows, :]
        for piece in range(start // half):
            cols = slice(piece * half, (piece + 1) * half)
            square = jnp.dot(feats, cen_ref[:, cols], preferred_element_type=jnp.float32)
            square = jnp.maximum(square, 1e-30)
            reach = square * lax.rsqrt(square)
            base = jnp.maximum(4.0 - reach, 0.0)
            base = base * base
            weight = (base * base * (reach + 1.0)).astype(jnp.bfloat16)
            part = jnp.dot(weight, coef_ref[cols, :], preferred_element_type=jnp.float32)
            part = part[:, 0:LANES]
            total = part if total is None else total + part
        if last:
            done_ref[rows, :] = total * (1.0 / 256.0)
            leave(index).start()
        else:
            out_ref[rows, :] = total
        return carry

    def over_tiles(body):
        if unrolled:
            for index in range(steps):
                body(index, 0)
        else:
            lax.fori_loop(0, steps, body, 0)

    unrolled = start // half <= UNROLLED
    over_tiles(step)
    if last:
        over_tiles(settle)


def vmem_specs(count):
    return [pl.BlockSpec(memory_space=pltpu.VMEM) for _ in range(count)]


def resident(value):
    return pltpu.with_memory_space_constraint(value, pltpu.VMEM)


def smem_specs(count):
    return [pl.BlockSpec(memory_space=pltpu.SMEM) for _ in range(count)]


def per_device(sens, dest_owner, dest_slot, coef_scale, centre_pos, node_pos, support):
    blocks = lax.axis_size("cblk")
    columns = lax.axis_size("nodes")
    row_count = sens.shape[0]
    groups = row_count // LANES
    half = blocks // 2 * LANES
    node_count = node_pos.shape[1]
    tile = 128
    me = lax.axis_index("cblk").astype(jnp.int32)[None]

    def swap(value, axis, size, mask):
        return lax.ppermute(value, axis, [(i, i ^ mask) for i in range(size)])

    params = pltpu.CompilerParams(vmem_limit_bytes=VMEM_LIMIT)
    extra = -(-(6 + 2 * groups) // EXTRA) * EXTRA
    meta = pl.pallas_call(
        meta_kernel,
        in_specs=[pl.BlockSpec(memory_space=pl.ANY)] * 4,
        out_specs=vmem_specs(1)[0],
        out_shape=pltpu.VMEM((extra, LANES), jnp.bfloat16),
        scratch_shapes=[
            pltpu.VMEM((groups, LANES), jnp.int32),
            pltpu.VMEM((groups, LANES), jnp.int32),
            pltpu.VMEM((1, LANES), jnp.float32),
            pltpu.VMEM(centre_pos.shape, jnp.bfloat16),
            pltpu.SemaphoreType.DMA((4,)),
        ],
        compiler_params=params,
        name="metadata",
    )(
        *[
            pltpu.with_memory_space_constraint(value, pltpu.HBM)
            for value in (
                dest_owner.reshape(groups, LANES),
                dest_slot.reshape(groups, LANES),
                coef_scale.reshape(1, LANES),
                centre_pos,
            )
        ]
    )
    feats = pl.pallas_call(
        functools.partial(feature_kernel, blocks=blocks),
        in_specs=smem_specs(2) + vmem_specs(1),
        out_specs=vmem_specs(1)[0],
        out_shape=pltpu.VMEM((node_count, DEPTH), jnp.bfloat16),
        compiler_params=params,
        cost_estimate=pl.CostEstimate(
            flops=node_count * 10000, transcendentals=0, bytes_accessed=node_count * 8
        ),
        name="features",
    )(me, support, node_pos)

    rows, metas, order = [sens], [meta], [0]
    mask = blocks // 2
    while mask:
        moved = [[swap(value, "cblk", blocks, mask) for value in part] for part in (rows, metas)]
        if mask == blocks // 2:
            moved, feats = lax.optimization_barrier((moved, feats))
        rows, metas = rows + moved[0], metas + moved[1]
        order = order + [s ^ mask for s in order]
        mask //= 2
    rows = [rows[order.index(s)] for s in range(blocks)]
    metas = [metas[order.index(s)] for s in range(blocks)]

    own, other = pl.pallas_call(
        functools.partial(coef_kernel, blocks=blocks, groups=groups),
        in_specs=smem_specs(1) + vmem_specs(2 * blocks),
        out_specs=vmem_specs(2),
        out_shape=[
            pltpu.VMEM((half + EXTRA, LANES), jnp.bfloat16),
            pltpu.VMEM((half, LANES), jnp.bfloat16),
        ],
        scratch_shapes=[pltpu.VMEM((blocks, extra, LANES), jnp.float32)],
        compiler_params=params,
        name="coefficients",
    )(me, *[resident(value) for value in rows + metas])

    stride = half + EXTRA

    def count_of(value):
        return value.shape[0] // stride

    def join(values):
        return pl.pallas_call(
            join_kernel,
            in_specs=vmem_specs(len(values)),
            out_specs=vmem_specs(1)[0],
            out_shape=pltpu.VMEM((stride * sum(count_of(v) for v in values), LANES), jnp.bfloat16),
            compiler_params=params,
            name="join",
        )(*[resident(value) for value in values])

    def morph(total, pieces, last=False):
        parts = tuple((count_of(chunk), side) for chunk, _, side in pieces)
        first = total is None
        operands = [feats] + ([] if first else [total])
        operands += [chunk for chunk, _, _ in pieces] + [value for _, value, _ in pieces]
        width = half * sum(count for count, _ in parts)
        work = node_count * width
        scratch = [
            pltpu.VMEM((DEPTH, width), jnp.bfloat16),
            pltpu.VMEM((width, 2 * LANES), jnp.bfloat16),
        ]
        if last:
            scratch += [
                pltpu.VMEM((node_count, LANES), jnp.float32),
                pltpu.SemaphoreType.DMA((node_count // tile,)),
            ]
        out = jax.ShapeDtypeStruct if last else pltpu.VMEM
        return pl.pallas_call(
            functools.partial(
                morph_kernel, blocks=blocks, parts=parts, first=first, last=last, tile=tile
            ),
            in_specs=vmem_specs(len(operands)),
            out_specs=pl.BlockSpec(memory_space=pl.ANY) if last else vmem_specs(1)[0],
            out_shape=out((node_count, LANES), jnp.float32),
            scratch_shapes=scratch,
            input_output_aliases={} if first or last else {1: 0},
            cost_estimate=pl.CostEstimate(
                flops=work * 600, transcendentals=work, bytes_accessed=node_count * LANES * 8
            ),
            compiler_params=pltpu.CompilerParams(vmem_limit_bytes=VMEM_LIMIT),
            name="morph",
        )(*[resident(value) for value in operands])

    def node_swap(value, mask):
        return swap(value, "nodes", columns, mask)

    def morph_both(total, values, last=False, split=True):
        others = [swap(value, "cblk", blocks, 1) for value in values]
        mine = [(value, value, 0) for value in values]
        theirs = [(value, out, 1) for value, out in zip(values, others)]
        if split:
            return morph(morph(total, mine), theirs, last)
        return morph(total, mine + theirs, last)

    mask = columns // 2
    have, ready, fresh, total = own, [], own, None
    while mask > 1:
        arrived = node_swap(have, mask)
        early = node_swap(fresh, 1)
        if total is None:
            total = morph(total, [(own, own, 0), (own, other, 1)])
        else:
            total = morph_both(total, ready, split=False)
        have, arrived, early, total = lax.optimization_barrier((have, arrived, early, total))
        ready, fresh = [arrived, early], arrived
        if mask > 2:
            have = join([have, arrived])
        mask //= 2
    late = node_swap(fresh, 1)
    total = morph_both(total, ready)
    late, total = lax.optimization_barrier((late, total))
    return morph_both(total, [late], True)


def solution(mesh):
    placed = (
        P(("nodes", "cblk"), None),
        P(("nodes", "cblk"), None),
        P(("nodes", "cblk")),
        P(("nodes", "cblk")),
        P(None, ("nodes", "cblk")),
        P(None, ("nodes", "cblk")),
        P(("nodes", "cblk"), None),
    )

    return jax.shard_map(
        per_device,
        mesh=mesh,
        in_specs=placed,
        out_specs=P(("nodes", "cblk"), None),
        check_vma=False,
    )
```

```python
import functools

import jax
import jax.numpy as jnp
from jax import lax
from jax.experimental import pallas as pl
from jax.experimental.pallas import tpu as pltpu
from jax.sharding import PartitionSpec as P


LANES = 128
EXTRA = 16
DEPTH = 32
FAR = 64.0
VMEM_LIMIT = 24 * 1024 * 1024
UNROLLED = 6
SUPPORT_RADIUS = 0.3
GAIN = 16.0 / (SUPPORT_RADIUS * SUPPORT_RADIUS)


def split3(value):
    high = value.astype(jnp.bfloat16).astype(jnp.float32)
    rest = value - high
    middle = rest.astype(jnp.bfloat16).astype(jnp.float32)
    return high, middle, rest - middle


def stack_rows(rows, width):
    rows = rows + [jnp.zeros((1, width), jnp.float32)] * (DEPTH - len(rows))
    return jnp.concatenate(rows, axis=0).astype(jnp.bfloat16)


def pack_kernel(*refs):
    sources, out_ref, targets, sems = refs[:5], refs[5], refs[6:10], refs[10]
    row_count = sources[0].shape[0]
    targets = (out_ref.at[pl.ds(0, row_count), :],) + targets
    copies = [
        pltpu.make_async_copy(source, target, sems.at[n])
        for n, (source, target) in enumerate(zip(sources, targets))
    ]
    for copy in copies:
        copy.start()
    for copy in copies[1:]:
        copy.wait()
    owner, slot, scale, pos = (target[...] for target in targets[1:])
    rows = [pos.astype(jnp.float32)] + list(split3(scale))
    rows += [owner.astype(jnp.float32), slot.astype(jnp.float32)]
    spare = out_ref.shape[0] - row_count - 6 - 2 * owner.shape[0]
    rows.append(jnp.zeros((spare, LANES), jnp.float32))
    out_ref[row_count:, :] = jnp.concatenate(rows, axis=0).astype(jnp.bfloat16)
    copies[0].wait()


def join_kernel(*refs):
    start = 0
    for ref in refs[:-1]:
        refs[-1][start : start + ref.shape[0], :] = ref[...]
        start += ref.shape[0]


def feature_kernel(me_ref, support_ref, pos_ref, out_ref, *, blocks):
    count = pos_ref.shape[1]
    tiles = support_ref.shape[0]
    width = count // tiles
    core = me_ref[0] & 1
    for tile in range(tiles):
        cols = pl.ds(tile * width, width)
        points = [pos_ref[k : k + 1, cols].astype(jnp.float32) for k in range(3)]
        norm = GAIN * (points[0] * points[0] + points[1] * points[1] + points[2] * points[2])
        ones = jnp.ones_like(norm)
        rows = points * 3 + list(split3(norm)) + [ones] * 3
        for k in range(blocks):
            place = lax.rem(core * (blocks // 2) + k, blocks)
            off = (1 - support_ref[tile, place]).astype(jnp.float32)
            rows.append(ones * off)
        out_ref[cols, :] = jnp.swapaxes(stack_rows(rows, width), 0, 1)


def coef_kernel(me_ref, *refs, blocks, groups):
    packs = refs[:blocks]
    own_ref, other_ref, metas = refs[blocks:]
    me = me_ref[0]
    core = me & 1
    half = blocks // 2 * LANES
    row_count = groups * LANES
    place = lax.broadcasted_iota(jnp.int32, (blocks * LANES, LANES), 0) + core * half
    place = (place & (blocks * LANES - 1)).astype(jnp.float32)
    sums = jnp.zeros((blocks * LANES, LANES), jnp.float32)
    for s in range(blocks):
        meta = packs[s][row_count:, :].astype(jnp.float32)
        metas[s] = meta
        target = meta[6 : 6 + groups, :] * LANES + meta[6 + groups : 6 + 2 * groups, :]
        picked = jnp.concatenate(
            [
                (place == target[g : g + 1, :]).astype(jnp.float32).astype(jnp.bfloat16)
                for g in range(groups)
            ],
            axis=1,
        )
        rows = packs[s][0:row_count, :]
        sums = sums + jnp.dot(picked, rows, preferred_element_type=jnp.float32)
    pos_rows = []
    for k in range(blocks):
        meta = metas[lax.rem(core * (blocks // 2) + k, blocks) ^ me]
        scale = meta[3:4, :] + meta[4:5, :] + meta[5:6, :]
        scale = jnp.swapaxes(jnp.broadcast_to(scale, (8, LANES)), 0, 1)[:, 0:1]
        coef = (scale * sums[k * LANES : (k + 1) * LANES, :]).astype(jnp.bfloat16)
        if k < blocks // 2:
            own_ref[k * LANES : (k + 1) * LANES, :] = coef
        else:
            other_ref[k * LANES - half : (k + 1) * LANES - half, :] = coef
        pos_rows.append(meta[0:3, :])
    pos_rows.append(jnp.zeros((EXTRA - 3 * blocks, LANES), jnp.float32))
    own_ref[half : half + EXTRA, :] = jnp.concatenate(pos_rows, axis=0).astype(jnp.bfloat16)


def centre_features(chunk_ref, row, side, blocks, out_ref, col):
    points = chunk_ref[row : row + EXTRA, :].astype(jnp.float32)
    for n in range(blocks // 2):
        k = side * (blocks // 2) + n
        pos = points[3 * k : 3 * k + 3, :]
        axes = [pos[d : d + 1, :] for d in range(3)]
        norm = GAIN * (axes[0] * axes[0] + axes[1] * axes[1] + axes[2] * axes[2])
        parts = [split3(-2.0 * GAIN * axis) for axis in axes]
        ones = jnp.ones_like(norm)
        rows = [parts[d][p] for p in range(3) for d in range(3)] + [ones] * 3 + list(split3(norm))
        rows += [ones * (FAR if k == b else 0.0) for b in range(blocks)]
        out_ref[:, col + n * LANES : col + (n + 1) * LANES] = stack_rows(rows, LANES)


def morph_kernel(*refs, blocks, parts, first, last, tile):
    feats_ref = refs[0]
    refs = refs[1:]
    if not first:
        acc_ref, refs = refs[0], refs[1:]
    arrays = len(parts)
    chunk_refs, value_refs = refs[:arrays], refs[arrays : 2 * arrays]
    out_ref, cen_ref, coef_ref = refs[2 * arrays : 2 * arrays + 3]
    if last:
        done_ref, sems = refs[2 * arrays + 3 :]
    half = blocks // 2 * LANES
    stride = half + EXTRA
    start = 0
    for (count, side), chunk_ref, value_ref in zip(parts, chunk_refs, value_refs):
        for n in range(count):
            centre_features(chunk_ref, n * stride + half, side, blocks, cen_ref, start)
            rows = slice(start, start + half)
            coef_ref[rows, 0:LANES] = value_ref[n * stride : n * stride + half, :]
            coef_ref[rows, LANES:] = jnp.zeros((half, LANES), jnp.bfloat16)
            start += half
    steps = feats_ref.shape[0] // tile

    def rows_of(index):
        return pl.ds(index * tile if unrolled else pl.multiple_of(index * tile, tile), tile)

    def leave(index):
        rows = rows_of(index)
        return pltpu.make_async_copy(done_ref.at[rows, :], out_ref.at[rows, :], sems.at[index])

    def settle(index, carry):
        leave(index).wait()
        return carry

    def step(index, carry):
        rows = rows_of(index)
        feats = feats_ref[rows, :]
        total = None if first else acc_ref[rows, :]
        for piece in range(start // half):
            cols = slice(piece * half, (piece + 1) * half)
            square = jnp.dot(feats, cen_ref[:, cols], preferred_element_type=jnp.float32)
            square = jnp.maximum(square, 1e-30)
            reach = square * lax.rsqrt(square)
            base = jnp.maximum(4.0 - reach, 0.0)
            base = base * base
            weight = (base * base * (reach + 1.0)).astype(jnp.bfloat16)
            part = jnp.dot(weight, coef_ref[cols, :], preferred_element_type=jnp.float32)
            part = part[:, 0:LANES]
            total = part if total is None else total + part
        if last:
            done_ref[rows, :] = total * (1.0 / 256.0)
            leave(index).start()
        else:
            out_ref[rows, :] = total
        return carry

    def over_tiles(body):
        if unrolled:
            for index in range(steps):
                body(index, 0)
        else:
            lax.fori_loop(0, steps, body, 0)

    unrolled = start // half <= UNROLLED
    over_tiles(step)
    if last:
        over_tiles(settle)


def vmem_specs(count):
    return [pl.BlockSpec(memory_space=pltpu.VMEM) for _ in range(count)]


def resident(value):
    return pltpu.with_memory_space_constraint(value, pltpu.VMEM)


def smem_specs(count):
    return [pl.BlockSpec(memory_space=pltpu.SMEM) for _ in range(count)]


def per_device(sens, dest_owner, dest_slot, coef_scale, centre_pos, node_pos, support):
    blocks = lax.axis_size("cblk")
    columns = lax.axis_size("nodes")
    row_count = sens.shape[0]
    groups = row_count // LANES
    half = blocks // 2 * LANES
    node_count = node_pos.shape[1]
    tile = 128
    me = lax.axis_index("cblk").astype(jnp.int32)[None]

    def swap(value, axis, size, mask):
        return lax.ppermute(value, axis, [(i, i ^ mask) for i in range(size)])

    params = pltpu.CompilerParams(vmem_limit_bytes=VMEM_LIMIT)
    extra = -(-(6 + 2 * groups) // EXTRA) * EXTRA
    pack = pl.pallas_call(
        pack_kernel,
        in_specs=[pl.BlockSpec(memory_space=pl.ANY)] * 5,
        out_specs=vmem_specs(1)[0],
        out_shape=pltpu.VMEM((row_count + extra, LANES), jnp.bfloat16),
        scratch_shapes=[
            pltpu.VMEM((groups, LANES), jnp.int32),
            pltpu.VMEM((groups, LANES), jnp.int32),
            pltpu.VMEM((1, LANES), jnp.float32),
            pltpu.VMEM(centre_pos.shape, jnp.bfloat16),
            pltpu.SemaphoreType.DMA((5,)),
        ],
        compiler_params=params,
        name="pack",
    )(
        *[
            pltpu.with_memory_space_constraint(value, pltpu.HBM)
            for value in (
                sens,
                dest_owner.reshape(groups, LANES),
                dest_slot.reshape(groups, LANES),
                coef_scale.reshape(1, LANES),
                centre_pos,
            )
        ]
    )
    feats = pl.pallas_call(
        functools.partial(feature_kernel, blocks=blocks),
        in_specs=smem_specs(2) + vmem_specs(1),
        out_specs=vmem_specs(1)[0],
        out_shape=pltpu.VMEM((node_count, DEPTH), jnp.bfloat16),
        compiler_params=params,
        cost_estimate=pl.CostEstimate(
            flops=node_count * 10000, transcendentals=0, bytes_accessed=node_count * 8
        ),
        name="features",
    )(me, support, node_pos)

    packs, order = [pack], [0]
    mask = blocks // 2
    while mask:
        arrived = [swap(value, "cblk", blocks, mask) for value in packs]
        if mask == blocks // 2:
            arrived, feats = lax.optimization_barrier((arrived, feats))
        packs = packs + arrived
        order = order + [s ^ mask for s in order]
        mask //= 2
    packs = [packs[order.index(s)] for s in range(blocks)]

    own, other = pl.pallas_call(
        functools.partial(coef_kernel, blocks=blocks, groups=groups),
        in_specs=smem_specs(1) + vmem_specs(blocks),
        out_specs=vmem_specs(2),
        out_shape=[
            pltpu.VMEM((half + EXTRA, LANES), jnp.bfloat16),
            pltpu.VMEM((half, LANES), jnp.bfloat16),
        ],
        scratch_shapes=[pltpu.VMEM((blocks, extra, LANES), jnp.float32)],
        compiler_params=params,
        name="coefficients",
    )(me, *[resident(value) for value in packs])

    stride = half + EXTRA

    def count_of(value):
        return value.shape[0] // stride

    def join(values):
        return pl.pallas_call(
            join_kernel,
            in_specs=vmem_specs(len(values)),
            out_specs=vmem_specs(1)[0],
            out_shape=pltpu.VMEM((stride * sum(count_of(v) for v in values), LANES), jnp.bfloat16),
            compiler_params=params,
            name="join",
        )(*[resident(value) for value in values])

    def morph(total, pieces, last=False):
        parts = tuple((count_of(chunk), side) for chunk, _, side in pieces)
        first = total is None
        operands = [feats] + ([] if first else [total])
        operands += [chunk for chunk, _, _ in pieces] + [value for _, value, _ in pieces]
        width = half * sum(count for count, _ in parts)
        work = node_count * width
        scratch = [
            pltpu.VMEM((DEPTH, width), jnp.bfloat16),
            pltpu.VMEM((width, 2 * LANES), jnp.bfloat16),
        ]
        if last:
            scratch += [
                pltpu.VMEM((node_count, LANES), jnp.float32),
                pltpu.SemaphoreType.DMA((node_count // tile,)),
            ]
        out = jax.ShapeDtypeStruct if last else pltpu.VMEM
        return pl.pallas_call(
            functools.partial(
                morph_kernel, blocks=blocks, parts=parts, first=first, last=last, tile=tile
            ),
            in_specs=vmem_specs(len(operands)),
            out_specs=pl.BlockSpec(memory_space=pl.ANY) if last else vmem_specs(1)[0],
            out_shape=out((node_count, LANES), jnp.float32),
            scratch_shapes=scratch,
            input_output_aliases={} if first or last else {1: 0},
            cost_estimate=pl.CostEstimate(
                flops=work * 600, transcendentals=work, bytes_accessed=node_count * LANES * 8
            ),
            compiler_params=pltpu.CompilerParams(vmem_limit_bytes=VMEM_LIMIT),
            name="morph",
        )(*[resident(value) for value in operands])

    def node_swap(value, mask):
        return swap(value, "nodes", columns, mask)

    def morph_both(total, values, last=False, split=True):
        value = join(values) if len(values) > 1 else values[0]
        mine, theirs = (value, value, 0), (value, swap(value, "cblk", blocks, 1), 1)
        if split:
            return morph(morph(total, [mine]), [theirs], last)
        return morph(total, [mine, theirs], last)

    mask = columns // 2
    have, ready, fresh, total = own, [], own, None
    while mask > 1:
        arrived = node_swap(have, mask)
        early = node_swap(fresh, 1)
        if total is None:
            total = morph(total, [(own, own, 0), (own, other, 1)])
        else:
            total = morph_both(total, ready, split=False)
        have, arrived, early, total = lax.optimization_barrier((have, arrived, early, total))
        ready, fresh = [arrived, early], arrived
        if mask > 2:
            have = join([have, arrived])
        mask //= 2
    late = node_swap(fresh, 1)
    total = morph_both(total, ready, split=False)
    late, total = lax.optimization_barrier((late, total))
    return morph_both(total, [late], True)


def solution(mesh):
    placed = (
        P(("nodes", "cblk"), None),
        P(("nodes", "cblk"), None),
        P(("nodes", "cblk")),
        P(("nodes", "cblk")),
        P(None, ("nodes", "cblk")),
        P(None, ("nodes", "cblk")),
        P(("nodes", "cblk"), None),
    )

    return jax.shard_map(
        per_device,
        mesh=mesh,
        in_specs=placed,
        out_specs=P(("nodes", "cblk"), None),
        check_vma=False,
    )
```

```python
import functools

import jax
import jax.numpy as jnp
from jax import lax
from jax.experimental import pallas as pl
from jax.experimental.pallas import tpu as pltpu
from jax.sharding import PartitionSpec as P


LANES = 128
EXTRA = 16
DEPTH = 32
FAR = 64.0
VMEM_LIMIT = 24 * 1024 * 1024
UNROLLED = 6
SUPPORT_RADIUS = 0.3
GAIN = 16.0 / (SUPPORT_RADIUS * SUPPORT_RADIUS)


def split3(value):
    high = value.astype(jnp.bfloat16).astype(jnp.float32)
    rest = value - high
    middle = rest.astype(jnp.bfloat16).astype(jnp.float32)
    return high, middle, rest - middle


def stack_rows(rows, width):
    rows = rows + [jnp.zeros((1, width), jnp.float32)] * (DEPTH - len(rows))
    return jnp.concatenate(rows, axis=0).astype(jnp.bfloat16)


def pack_kernel(*refs):
    sources, out_ref, targets, sems = refs[:5], refs[5], refs[6:10], refs[10]
    row_count = sources[0].shape[0]
    targets = (out_ref.at[pl.ds(0, row_count), :],) + targets
    copies = [
        pltpu.make_async_copy(source, target, sems.at[n])
        for n, (source, target) in enumerate(zip(sources, targets))
    ]
    for copy in copies:
        copy.start()
    for copy in copies[1:]:
        copy.wait()
    owner, slot, scale, pos = (target[...] for target in targets[1:])
    rows = [pos.astype(jnp.float32)] + list(split3(scale))
    rows += [owner.astype(jnp.float32), slot.astype(jnp.float32)]
    spare = out_ref.shape[0] - row_count - 6 - 2 * owner.shape[0]
    rows.append(jnp.zeros((spare, LANES), jnp.float32))
    out_ref[row_count:, :] = jnp.concatenate(rows, axis=0).astype(jnp.bfloat16)
    copies[0].wait()


def join_kernel(*refs):
    start = 0
    for ref in refs[:-1]:
        refs[-1][start : start + ref.shape[0], :] = ref[...]
        start += ref.shape[0]


def feature_kernel(me_ref, support_ref, pos_ref, out_ref, *, blocks):
    count = pos_ref.shape[1]
    tiles = support_ref.shape[0]
    width = count // tiles
    core = me_ref[0] & 1
    for tile in range(tiles):
        cols = pl.ds(tile * width, width)
        points = [pos_ref[k : k + 1, cols].astype(jnp.float32) for k in range(3)]
        norm = GAIN * (points[0] * points[0] + points[1] * points[1] + points[2] * points[2])
        ones = jnp.ones_like(norm)
        rows = points * 3 + list(split3(norm)) + [ones] * 3
        for k in range(blocks):
            place = lax.rem(core * (blocks // 2) + k, blocks)
            off = (1 - support_ref[tile, place]).astype(jnp.float32)
            rows.append(ones * off)
        out_ref[cols, :] = jnp.swapaxes(stack_rows(rows, width), 0, 1)


def add_hits(me_ref, packs, metas, sums, groups, blocks, side):
    half = blocks // 2 * LANES
    row_count = groups * LANES
    place = lax.broadcasted_iota(jnp.int32, (half, LANES), 0) + ((me_ref[0] & 1) + side) * half
    place = (place & (blocks * LANES - 1)).astype(jnp.float32)
    for s, pack in packs:
        meta = pack[row_count:, :].astype(jnp.float32)
        metas[s] = meta
        target = meta[6 : 6 + groups, :] * LANES + meta[6 + groups : 6 + 2 * groups, :]
        picked = jnp.concatenate(
            [
                (place == target[g : g + 1, :]).astype(jnp.float32).astype(jnp.bfloat16)
                for g in range(groups)
            ],
            axis=1,
        )
        rows = pack[0:row_count, :]
        part = jnp.dot(picked, rows, preferred_element_type=jnp.float32)
        sums = part if sums is None else sums + part
    return sums


def early_kernel(me_ref, *refs, blocks, groups, places):
    packs, (out_ref, metas) = refs[: len(places)], refs[len(places) :]
    out_ref[...] = add_hits(me_ref, list(zip(places, packs)), metas, None, groups, blocks, 0)


def coef_kernel(me_ref, sums_ref, *refs, blocks, groups, side, places):
    packs = refs[:blocks]
    out_ref, metas = refs[blocks:]
    me = me_ref[0]
    core = me & 1
    half = blocks // 2 * LANES
    sums = None
    if side == 0:
        sums = sums_ref[...]
        for s in range(blocks):
            metas[s] = packs[s][groups * LANES :, :].astype(jnp.float32)
    wanted = [(s, packs[s]) for s in range(blocks) if side or s not in places]
    sums = add_hits(me_ref, wanted, metas, sums, groups, blocks, side)

    def meta_of(k):
        return metas[lax.rem(core * (blocks // 2) + k, blocks) ^ me]

    for n in range(blocks // 2):
        meta = meta_of(side * (blocks // 2) + n)
        scale = meta[3:4, :] + meta[4:5, :] + meta[5:6, :]
        scale = jnp.swapaxes(jnp.broadcast_to(scale, (8, LANES)), 0, 1)[:, 0:1]
        rows = slice(n * LANES, (n + 1) * LANES)
        out_ref[rows, :] = (scale * sums[rows, :]).astype(jnp.bfloat16)
    if side == 0:
        pos_rows = [meta_of(k)[0:3, :] for k in range(blocks)]
        pos_rows.append(jnp.zeros((EXTRA - 3 * blocks, LANES), jnp.float32))
        out_ref[half:, :] = jnp.concatenate(pos_rows, axis=0).astype(jnp.bfloat16)


def centre_features(chunk_ref, row, side, blocks, out_ref, col):
    points = chunk_ref[row : row + EXTRA, :].astype(jnp.float32)
    for n in range(blocks // 2):
        k = side * (blocks // 2) + n
        pos = points[3 * k : 3 * k + 3, :]
        axes = [pos[d : d + 1, :] for d in range(3)]
        norm = GAIN * (axes[0] * axes[0] + axes[1] * axes[1] + axes[2] * axes[2])
        parts = [split3(-2.0 * GAIN * axis) for axis in axes]
        ones = jnp.ones_like(norm)
        rows = [parts[d][p] for p in range(3) for d in range(3)] + [ones] * 3 + list(split3(norm))
        rows += [ones * (FAR if k == b else 0.0) for b in range(blocks)]
        out_ref[:, col + n * LANES : col + (n + 1) * LANES] = stack_rows(rows, LANES)


def morph_kernel(*refs, blocks, parts, first, last, tile):
    feats_ref = refs[0]
    refs = refs[1:]
    if not first:
        acc_ref, refs = refs[0], refs[1:]
    arrays = len(parts)
    chunk_refs, value_refs = refs[:arrays], refs[arrays : 2 * arrays]
    out_ref, cen_ref, coef_ref = refs[2 * arrays : 2 * arrays + 3]
    if last:
        done_ref, sems = refs[2 * arrays + 3 :]
    half = blocks // 2 * LANES
    stride = half + EXTRA
    start = 0
    for (count, side), chunk_ref, value_ref in zip(parts, chunk_refs, value_refs):
        for n in range(count):
            centre_features(chunk_ref, n * stride + half, side, blocks, cen_ref, start)
            rows = slice(start, start + half)
            coef_ref[rows, 0:LANES] = value_ref[n * stride : n * stride + half, :]
            coef_ref[rows, LANES:] = jnp.zeros((half, LANES), jnp.bfloat16)
            start += half
    steps = feats_ref.shape[0] // tile

    def rows_of(index):
        return pl.ds(index * tile if unrolled else pl.multiple_of(index * tile, tile), tile)

    def leave(index):
        rows = rows_of(index)
        return pltpu.make_async_copy(done_ref.at[rows, :], out_ref.at[rows, :], sems.at[index])

    def settle(index, carry):
        leave(index).wait()
        return carry

    def step(index, carry):
        rows = rows_of(index)
        feats = feats_ref[rows, :]
        total = None if first else acc_ref[rows, :]
        for piece in range(start // half):
            cols = slice(piece * half, (piece + 1) * half)
            square = jnp.dot(feats, cen_ref[:, cols], preferred_element_type=jnp.float32)
            square = jnp.maximum(square, 1e-30)
            reach = square * lax.rsqrt(square)
            base = jnp.maximum(4.0 - reach, 0.0)
            base = base * base
            weight = (base * base * (reach + 1.0)).astype(jnp.bfloat16)
            part = jnp.dot(weight, coef_ref[cols, :], preferred_element_type=jnp.float32)
            part = part[:, 0:LANES]
            total = part if total is None else total + part
        if last:
            done_ref[rows, :] = total * (1.0 / 256.0)
            leave(index).start()
        else:
            out_ref[rows, :] = total
        return carry

    def over_tiles(body):
        if unrolled:
            for index in range(steps):
                body(index, 0)
        else:
            lax.fori_loop(0, steps, body, 0)

    unrolled = start // half <= UNROLLED
    over_tiles(step)
    if last:
        over_tiles(settle)


def vmem_specs(count):
    return [pl.BlockSpec(memory_space=pltpu.VMEM) for _ in range(count)]


def resident(value):
    return pltpu.with_memory_space_constraint(value, pltpu.VMEM)


def smem_specs(count):
    return [pl.BlockSpec(memory_space=pltpu.SMEM) for _ in range(count)]


def per_device(sens, dest_owner, dest_slot, coef_scale, centre_pos, node_pos, support):
    blocks = lax.axis_size("cblk")
    columns = lax.axis_size("nodes")
    row_count = sens.shape[0]
    groups = row_count // LANES
    half = blocks // 2 * LANES
    node_count = node_pos.shape[1]
    tile = 128
    me = lax.axis_index("cblk").astype(jnp.int32)[None]

    def swap(value, axis, size, mask):
        return lax.ppermute(value, axis, [(i, i ^ mask) for i in range(size)])

    params = pltpu.CompilerParams(vmem_limit_bytes=VMEM_LIMIT)
    extra = -(-(6 + 2 * groups) // EXTRA) * EXTRA
    pack = pl.pallas_call(
        pack_kernel,
        in_specs=[pl.BlockSpec(memory_space=pl.ANY)] * 5,
        out_specs=vmem_specs(1)[0],
        out_shape=pltpu.VMEM((row_count + extra, LANES), jnp.bfloat16),
        scratch_shapes=[
            pltpu.VMEM((groups, LANES), jnp.int32),
            pltpu.VMEM((groups, LANES), jnp.int32),
            pltpu.VMEM((1, LANES), jnp.float32),
            pltpu.VMEM(centre_pos.shape, jnp.bfloat16),
            pltpu.SemaphoreType.DMA((5,)),
        ],
        compiler_params=params,
        name="pack",
    )(
        *[
            pltpu.with_memory_space_constraint(value, pltpu.HBM)
            for value in (
                sens,
                dest_owner.reshape(groups, LANES),
                dest_slot.reshape(groups, LANES),
                coef_scale.reshape(1, LANES),
                centre_pos,
            )
        ]
    )
    feats = pl.pallas_call(
        functools.partial(feature_kernel, blocks=blocks),
        in_specs=smem_specs(2) + vmem_specs(1),
        out_specs=vmem_specs(1)[0],
        out_shape=pltpu.VMEM((node_count, DEPTH), jnp.bfloat16),
        compiler_params=params,
        cost_estimate=pl.CostEstimate(
            flops=node_count * 10000, transcendentals=0, bytes_accessed=node_count * 8
        ),
        name="features",
    )(me, support, node_pos)

    packs, order = [pack], [0]
    mask = blocks // 2
    while mask:
        arrived = [swap(value, "cblk", blocks, mask) for value in packs]
        if mask == blocks // 2:
            arrived, feats = lax.optimization_barrier((arrived, feats))
        packs = packs + arrived
        order = order + [s ^ mask for s in order]
        mask //= 2
    packs = [packs[order.index(s)] for s in range(blocks)]

    places = (0, blocks // 2)
    sums = pl.pallas_call(
        functools.partial(early_kernel, blocks=blocks, groups=groups, places=places),
        in_specs=smem_specs(1) + vmem_specs(2),
        out_specs=vmem_specs(1)[0],
        out_shape=pltpu.VMEM((half, LANES), jnp.float32),
        scratch_shapes=[pltpu.VMEM((blocks, extra, LANES), jnp.float32)],
        compiler_params=params,
        name="early_sums",
    )(me, *[resident(packs[place]) for place in places])

    def coefficients(side, out_rows):
        return pl.pallas_call(
            functools.partial(
                coef_kernel, blocks=blocks, groups=groups, side=side, places=places
            ),
            in_specs=smem_specs(1) + vmem_specs(1 + blocks),
            out_specs=vmem_specs(1)[0],
            out_shape=pltpu.VMEM((out_rows, LANES), jnp.bfloat16),
            scratch_shapes=[pltpu.VMEM((blocks, extra, LANES), jnp.float32)],
            compiler_params=params,
            name="coefficients",
        )(me, resident(sums), *[resident(value) for value in packs])

    own, other = coefficients(0, half + EXTRA), coefficients(1, half)

    stride = half + EXTRA

    def count_of(value):
        return value.shape[0] // stride

    def join(values):
        return pl.pallas_call(
            join_kernel,
            in_specs=vmem_specs(len(values)),
            out_specs=vmem_specs(1)[0],
            out_shape=pltpu.VMEM((stride * sum(count_of(v) for v in values), LANES), jnp.bfloat16),
            compiler_params=params,
            name="join",
        )(*[resident(value) for value in values])

    def morph(total, pieces, last=False):
        parts = tuple((count_of(chunk), side) for chunk, _, side in pieces)
        first = total is None
        operands = [feats] + ([] if first else [total])
        operands += [chunk for chunk, _, _ in pieces] + [value for _, value, _ in pieces]
        width = half * sum(count for count, _ in parts)
        work = node_count * width
        scratch = [
            pltpu.VMEM((DEPTH, width), jnp.bfloat16),
            pltpu.VMEM((width, 2 * LANES), jnp.bfloat16),
        ]
        if last:
            scratch += [
                pltpu.VMEM((node_count, LANES), jnp.float32),
                pltpu.SemaphoreType.DMA((node_count // tile,)),
            ]
        out = jax.ShapeDtypeStruct if last else pltpu.VMEM
        return pl.pallas_call(
            functools.partial(
                morph_kernel, blocks=blocks, parts=parts, first=first, last=last, tile=tile
            ),
            in_specs=vmem_specs(len(operands)),
            out_specs=pl.BlockSpec(memory_space=pl.ANY) if last else vmem_specs(1)[0],
            out_shape=out((node_count, LANES), jnp.float32),
            scratch_shapes=scratch,
            input_output_aliases={} if first or last else {1: 0},
            cost_estimate=pl.CostEstimate(
                flops=work * 600, transcendentals=work, bytes_accessed=node_count * LANES * 8
            ),
            compiler_params=pltpu.CompilerParams(vmem_limit_bytes=VMEM_LIMIT),
            name="morph",
        )(*[resident(value) for value in operands])

    def node_swap(value, mask):
        return swap(value, "nodes", columns, mask)

    def morph_both(total, values, last=False, split=True):
        value = join(values) if len(values) > 1 else values[0]
        mine, theirs = (value, value, 0), (value, swap(value, "cblk", blocks, 1), 1)
        if split:
            return morph(morph(total, [mine]), [theirs], last)
        return morph(total, [mine, theirs], last)

    mask = columns // 2
    have, ready, fresh, total = own, [], own, None
    while mask > 1:
        arrived = node_swap(have, mask)
        early = node_swap(fresh, 1)
        if total is None:
            total = morph(total, [(own, own, 0), (own, other, 1)])
        else:
            total = morph_both(total, ready, split=False)
        have, arrived, early, total = lax.optimization_barrier((have, arrived, early, total))
        ready, fresh = [arrived, early], arrived
        if mask > 2:
            have = join([have, arrived])
        mask //= 2
    late = node_swap(fresh, 1)
    total = morph_both(total, ready, split=False)
    late, total = lax.optimization_barrier((late, total))
    return morph_both(total, [late], True)


def solution(mesh):
    placed = (
        P(("nodes", "cblk"), None),
        P(("nodes", "cblk"), None),
        P(("nodes", "cblk")),
        P(("nodes", "cblk")),
        P(None, ("nodes", "cblk")),
        P(None, ("nodes", "cblk")),
        P(("nodes", "cblk"), None),
    )

    return jax.shard_map(
        per_device,
        mesh=mesh,
        in_specs=placed,
        out_specs=P(("nodes", "cblk"), None),
        check_vma=False,
    )
```

```python
import functools

import jax
import jax.numpy as jnp
from jax import lax
from jax.experimental import pallas as pl
from jax.experimental.pallas import tpu as pltpu
from jax.sharding import PartitionSpec as P


LANES = 128
EXTRA = 16
DEPTH = 32
FAR = 64.0
VMEM_LIMIT = 24 * 1024 * 1024
UNROLLED = 6
SUPPORT_RADIUS = 0.3
GAIN = 16.0 / (SUPPORT_RADIUS * SUPPORT_RADIUS)


def split3(value):
    high = value.astype(jnp.bfloat16).astype(jnp.float32)
    rest = value - high
    middle = rest.astype(jnp.bfloat16).astype(jnp.float32)
    return high, middle, rest - middle


def stack_rows(rows, width):
    rows = rows + [jnp.zeros((1, width), jnp.float32)] * (DEPTH - len(rows))
    return jnp.concatenate(rows, axis=0).astype(jnp.bfloat16)


def pack_kernel(*refs):
    sources, out_ref, targets, sems = refs[:5], refs[5], refs[6:10], refs[10]
    row_count = sources[0].shape[0]
    targets = (out_ref.at[pl.ds(0, row_count), :],) + targets
    copies = [
        pltpu.make_async_copy(source, target, sems.at[n])
        for n, (source, target) in enumerate(zip(sources, targets))
    ]
    for copy in copies:
        copy.start()
    for copy in copies[1:]:
        copy.wait()
    owner, slot, scale, pos = (target[...] for target in targets[1:])
    rows = [pos.astype(jnp.float32)] + list(split3(scale))
    rows += [owner.astype(jnp.float32), slot.astype(jnp.float32)]
    spare = out_ref.shape[0] - row_count - 6 - 2 * owner.shape[0]
    rows.append(jnp.zeros((spare, LANES), jnp.float32))
    out_ref[row_count:, :] = jnp.concatenate(rows, axis=0).astype(jnp.bfloat16)
    copies[0].wait()


def join_kernel(*refs):
    start = 0
    for ref in refs[:-1]:
        refs[-1][start : start + ref.shape[0], :] = ref[...]
        start += ref.shape[0]


def feature_kernel(me_ref, support_ref, pos_ref, out_ref, *, blocks):
    count = pos_ref.shape[1]
    tiles = support_ref.shape[0]
    width = count // tiles
    core = me_ref[0] & 1
    for tile in range(tiles):
        cols = pl.ds(tile * width, width)
        points = [pos_ref[k : k + 1, cols].astype(jnp.float32) for k in range(3)]
        norm = GAIN * (points[0] * points[0] + points[1] * points[1] + points[2] * points[2])
        ones = jnp.ones_like(norm)
        rows = points * 3 + list(split3(norm)) + [ones] * 3
        for k in range(blocks):
            place = lax.rem(core * (blocks // 2) + k, blocks)
            off = (1 - support_ref[tile, place]).astype(jnp.float32)
            rows.append(ones * off)
        out_ref[cols, :] = jnp.swapaxes(stack_rows(rows, width), 0, 1)


def coef_kernel(me_ref, *refs, blocks, groups, side):
    packs = refs[:blocks]
    out_ref, metas = refs[blocks:]
    me = me_ref[0]
    core = me & 1
    half = blocks // 2 * LANES
    row_count = groups * LANES
    place = lax.broadcasted_iota(jnp.int32, (half, LANES), 0) + (core + side) * half
    place = (place & (blocks * LANES - 1)).astype(jnp.float32)
    sums = jnp.zeros((half, LANES), jnp.float32)
    for s in range(blocks):
        meta = packs[s][row_count:, :].astype(jnp.float32)
        metas[s] = meta
        target = meta[6 : 6 + groups, :] * LANES + meta[6 + groups : 6 + 2 * groups, :]
        picked = jnp.concatenate(
            [
                (place == target[g : g + 1, :]).astype(jnp.float32).astype(jnp.bfloat16)
                for g in range(groups)
            ],
            axis=1,
        )
        rows = packs[s][0:row_count, :]
        sums = sums + jnp.dot(picked, rows, preferred_element_type=jnp.float32)

    def meta_of(k):
        return metas[lax.rem(core * (blocks // 2) + k, blocks) ^ me]

    for n in range(blocks // 2):
        meta = meta_of(side * (blocks // 2) + n)
        scale = meta[3:4, :] + meta[4:5, :] + meta[5:6, :]
        scale = jnp.swapaxes(jnp.broadcast_to(scale, (8, LANES)), 0, 1)[:, 0:1]
        rows = slice(n * LANES, (n + 1) * LANES)
        out_ref[rows, :] = (scale * sums[rows, :]).astype(jnp.bfloat16)
    if side == 0:
        pos_rows = [meta_of(k)[0:3, :] for k in range(blocks)]
        pos_rows.append(jnp.zeros((EXTRA - 3 * blocks, LANES), jnp.float32))
        out_ref[half:, :] = jnp.concatenate(pos_rows, axis=0).astype(jnp.bfloat16)


def centre_features(chunk_ref, row, side, blocks, out_ref, col):
    points = chunk_ref[row : row + EXTRA, :].astype(jnp.float32)
    for n in range(blocks // 2):
        k = side * (blocks // 2) + n
        pos = points[3 * k : 3 * k + 3, :]
        axes = [pos[d : d + 1, :] for d in range(3)]
        norm = GAIN * (axes[0] * axes[0] + axes[1] * axes[1] + axes[2] * axes[2])
        parts = [split3(-2.0 * GAIN * axis) for axis in axes]
        ones = jnp.ones_like(norm)
        rows = [parts[d][p] for p in range(3) for d in range(3)] + [ones] * 3 + list(split3(norm))
        rows += [ones * (FAR if k == b else 0.0) for b in range(blocks)]
        out_ref[:, col + n * LANES : col + (n + 1) * LANES] = stack_rows(rows, LANES)


def morph_kernel(*refs, blocks, parts, first, last, tile):
    feats_ref = refs[0]
    refs = refs[1:]
    if not first:
        acc_ref, refs = refs[0], refs[1:]
    arrays = len(parts)
    chunk_refs, value_refs = refs[:arrays], refs[arrays : 2 * arrays]
    out_ref, cen_ref, coef_ref = refs[2 * arrays : 2 * arrays + 3]
    if last:
        done_ref, sems = refs[2 * arrays + 3 :]
    half = blocks // 2 * LANES
    stride = half + EXTRA
    start = 0
    for (count, side), chunk_ref, value_ref in zip(parts, chunk_refs, value_refs):
        for n in range(count):
            centre_features(chunk_ref, n * stride + half, side, blocks, cen_ref, start)
            rows = slice(start, start + half)
            coef_ref[rows, 0:LANES] = value_ref[n * stride : n * stride + half, :]
            coef_ref[rows, LANES:] = jnp.zeros((half, LANES), jnp.bfloat16)
            start += half
    steps = feats_ref.shape[0] // tile

    def rows_of(index):
        return pl.ds(index * tile if unrolled else pl.multiple_of(index * tile, tile), tile)

    def leave(index):
        rows = rows_of(index)
        return pltpu.make_async_copy(done_ref.at[rows, :], out_ref.at[rows, :], sems.at[index])

    def settle(index, carry):
        leave(index).wait()
        return carry

    def step(index, carry):
        rows = rows_of(index)
        feats = feats_ref[rows, :]
        total = None if first else acc_ref[rows, :]
        for piece in range(start // half):
            cols = slice(piece * half, (piece + 1) * half)
            square = jnp.dot(feats, cen_ref[:, cols], preferred_element_type=jnp.float32)
            square = jnp.maximum(square, 1e-30)
            reach = square * lax.rsqrt(square)
            base = jnp.maximum(4.0 - reach, 0.0)
            base = base * base
            weight = (base * base * (reach + 1.0)).astype(jnp.bfloat16)
            part = jnp.dot(weight, coef_ref[cols, :], preferred_element_type=jnp.float32)
            part = part[:, 0:LANES]
            total = part if total is None else total + part
        if last:
            done_ref[rows, :] = total * (1.0 / 256.0)
            leave(index).start()
        else:
            out_ref[rows, :] = total
        return carry

    def over_tiles(body):
        if unrolled:
            for index in range(steps):
                body(index, 0)
        else:
            lax.fori_loop(0, steps, body, 0)

    unrolled = start // half <= UNROLLED
    over_tiles(step)
    if last:
        over_tiles(settle)


def vmem_specs(count):
    return [pl.BlockSpec(memory_space=pltpu.VMEM) for _ in range(count)]


def resident(value):
    return pltpu.with_memory_space_constraint(value, pltpu.VMEM)


def smem_specs(count):
    return [pl.BlockSpec(memory_space=pltpu.SMEM) for _ in range(count)]


def per_device(sens, dest_owner, dest_slot, coef_scale, centre_pos, node_pos, support):
    blocks = lax.axis_size("cblk")
    columns = lax.axis_size("nodes")
    row_count = sens.shape[0]
    groups = row_count // LANES
    half = blocks // 2 * LANES
    node_count = node_pos.shape[1]
    tile = 128
    me = lax.axis_index("cblk").astype(jnp.int32)[None]

    def swap(value, axis, size, mask):
        return lax.ppermute(value, axis, [(i, i ^ mask) for i in range(size)])

    params = pltpu.CompilerParams(vmem_limit_bytes=VMEM_LIMIT)
    extra = -(-(6 + 2 * groups) // EXTRA) * EXTRA
    pack = pl.pallas_call(
        pack_kernel,
        in_specs=[pl.BlockSpec(memory_space=pl.ANY)] * 5,
        out_specs=vmem_specs(1)[0],
        out_shape=pltpu.VMEM((row_count + extra, LANES), jnp.bfloat16),
        scratch_shapes=[
            pltpu.VMEM((groups, LANES), jnp.int32),
            pltpu.VMEM((groups, LANES), jnp.int32),
            pltpu.VMEM((1, LANES), jnp.float32),
            pltpu.VMEM(centre_pos.shape, jnp.bfloat16),
            pltpu.SemaphoreType.DMA((5,)),
        ],
        compiler_params=params,
        name="pack",
    )(
        *[
            pltpu.with_memory_space_constraint(value, pltpu.HBM)
            for value in (
                sens,
                dest_owner.reshape(groups, LANES),
                dest_slot.reshape(groups, LANES),
                coef_scale.reshape(1, LANES),
                centre_pos,
            )
        ]
    )
    feats = pl.pallas_call(
        functools.partial(feature_kernel, blocks=blocks),
        in_specs=smem_specs(2) + vmem_specs(1),
        out_specs=vmem_specs(1)[0],
        out_shape=pltpu.VMEM((node_count, DEPTH), jnp.bfloat16),
        compiler_params=params,
        cost_estimate=pl.CostEstimate(
            flops=node_count * 10000, transcendentals=0, bytes_accessed=node_count * 8
        ),
        name="features",
    )(me, support, node_pos)

    packs, order = [pack], [0]
    mask = blocks // 2
    while mask:
        arrived = [swap(value, "cblk", blocks, mask) for value in packs]
        if mask == blocks // 2:
            arrived, feats = lax.optimization_barrier((arrived, feats))
        packs = packs + arrived
        order = order + [s ^ mask for s in order]
        mask //= 2
    packs = [packs[order.index(s)] for s in range(blocks)]

    def coefficients(side, out_rows):
        return pl.pallas_call(
            functools.partial(coef_kernel, blocks=blocks, groups=groups, side=side),
            in_specs=smem_specs(1) + vmem_specs(blocks),
            out_specs=vmem_specs(1)[0],
            out_shape=pltpu.VMEM((out_rows, LANES), jnp.bfloat16),
            scratch_shapes=[pltpu.VMEM((blocks, extra, LANES), jnp.float32)],
            compiler_params=params,
            name="coefficients",
        )(me, *[resident(value) for value in packs])

    own, other = coefficients(0, half + EXTRA), coefficients(1, half)

    stride = half + EXTRA

    def count_of(value):
        return value.shape[0] // stride

    def join(values):
        return pl.pallas_call(
            join_kernel,
            in_specs=vmem_specs(len(values)),
            out_specs=vmem_specs(1)[0],
            out_shape=pltpu.VMEM((stride * sum(count_of(v) for v in values), LANES), jnp.bfloat16),
            compiler_params=params,
            name="join",
        )(*[resident(value) for value in values])

    def morph(total, pieces, last=False):
        parts = tuple((count_of(chunk), side) for chunk, _, side in pieces)
        first = total is None
        operands = [feats] + ([] if first else [total])
        operands += [chunk for chunk, _, _ in pieces] + [value for _, value, _ in pieces]
        width = half * sum(count for count, _ in parts)
        work = node_count * width
        scratch = [
            pltpu.VMEM((DEPTH, width), jnp.bfloat16),
            pltpu.VMEM((width, 2 * LANES), jnp.bfloat16),
        ]
        if last:
            scratch += [
                pltpu.VMEM((node_count, LANES), jnp.float32),
                pltpu.SemaphoreType.DMA((node_count // tile,)),
            ]
        out = jax.ShapeDtypeStruct if last else pltpu.VMEM
        return pl.pallas_call(
            functools.partial(
                morph_kernel, blocks=blocks, parts=parts, first=first, last=last, tile=tile
            ),
            in_specs=vmem_specs(len(operands)),
            out_specs=pl.BlockSpec(memory_space=pl.ANY) if last else vmem_specs(1)[0],
            out_shape=out((node_count, LANES), jnp.float32),
            scratch_shapes=scratch,
            input_output_aliases={} if first or last else {1: 0},
            cost_estimate=pl.CostEstimate(
                flops=work * 600, transcendentals=work, bytes_accessed=node_count * LANES * 8
            ),
            compiler_params=params,
            name="morph",
        )(*[resident(value) for value in operands])

    def node_swap(value, mask):
        return swap(value, "nodes", columns, mask)

    def morph_both(total, values, last=False, split=True):
        value = join(values) if len(values) > 1 else values[0]
        mine, theirs = (value, value, 0), (value, swap(value, "cblk", blocks, 1), 1)
        if split:
            return morph(morph(total, [mine]), [theirs], last)
        return morph(total, [mine, theirs], last)

    mask = columns // 2
    have, ready, fresh, total = own, [], own, None
    while mask > 1:
        arrived = node_swap(have, mask)
        early = node_swap(fresh, 1)
        if total is None:
            total = morph(total, [(own, own, 0), (own, other, 1)])
        else:
            total = morph_both(total, ready, split=False)
        have, arrived, early, total = lax.optimization_barrier((have, arrived, early, total))
        ready, fresh = [arrived, early], arrived
        if mask > 2:
            have = join([have, arrived])
        mask //= 2
    late = node_swap(fresh, 1)
    total = morph_both(total, ready, split=False)
    late, total = lax.optimization_barrier((late, total))
    return morph_both(total, [late], True)


def solution(mesh):
    placed = (
        P(("nodes", "cblk"), None),
        P(("nodes", "cblk"), None),
        P(("nodes", "cblk")),
        P(("nodes", "cblk")),
        P(None, ("nodes", "cblk")),
        P(None, ("nodes", "cblk")),
        P(("nodes", "cblk"), None),
    )

    return jax.shard_map(
        per_device,
        mesh=mesh,
        in_specs=placed,
        out_specs=P(("nodes", "cblk"), None),
        check_vma=False,
    )
```
